256 devices in a mesh: seq: 16 (over x, y_lo, core), ch: 16 (over z, y_hi).
Axes of the slice: x: 4, y: 4 (y_hi: 2, y_lo: 2; y = y_hi * 2 + y_lo), z: 8, core: 2. Of those that a mesh axis runs over, the one named last changes fastest.
Arguments:
- grad_out: bfloat16 [2048, 8192], P('seq', 'ch'), may hold values from -6 to 6
- out_weight: bfloat16 [8192, 8192], P('ch'), may hold values from -0.0625 to 0.0625
- query_gate: bfloat16 [2048, 8192], P('seq', 'ch'), may hold values from -6 to 6
- key_branch: bfloat16 [2048, 8192], P('seq', 'ch'), may hold values from -6 to 6
- value_branch: bfloat16 [2048, 8192], P('seq', 'ch'), may hold values from -6 to 6
- filter_taps: bfloat16 [2048, 8192], P('seq', 'ch'), may hold values from -4 to 4
Outputs:
- key_grad: bfloat16 [2048, 8192], P('seq', 'ch')
- value_grad: bfloat16 [2048, 8192], P('seq', 'ch')
- filter_grad: float32 [2048, 8192], P('seq', 'ch')
The draws below stay inside these ranges and needn't reach their ends.
All inputs are finite; a program needn't handle non-finite values.
Results may differ from the reference program's by a relative error of at most 0.017.
Values may be sent and summed in bfloat16 or wider, within the bound.
A program may use at most 192 MiB of HBM per device.

```python
import math
import jax
import jax.numpy as jnp
from jax import lax

D = 8192
LS = 128
SEQ = 2048
N_SEQ = 16


def draw_filter_taps(key, part):
    rate_key, noise_key = jax.random.split(jax.random.fold_in(key, 17))
    fraction = jax.random.uniform(rate_key, (1, D), jnp.float32)
    lag_index = jnp.arange(SEQ, dtype=jnp.float32)[:, None]
    log_low = math.log(LS / 4.0)
    log_high = math.log(2.0 * SEQ)
    noise_part = jnp.clip(jax.random.normal(noise_key, (SEQ, D), jnp.float32), -4.0, 4.0)
    reach_len = jnp.exp(log_low + fraction * (log_high - log_low))
    return (noise_part * jnp.sqrt(2.0 / reach_len) * jnp.exp(-lag_index / reach_len)).astype(jnp.bfloat16)


def block_scale(stream_key, extent, pieces, low, high):
    factor_of = 1.0
    for axis_at, blocks in pieces:
        steps = jax.random.uniform(jax.random.fold_in(jax.random.fold_in(stream_key, 6), axis_at), (blocks,), jnp.float32, low / len(pieces), high / len(pieces))
        factor_of = factor_of * jnp.repeat(jnp.exp(steps), extent[axis_at] // blocks).reshape((-1,) + (1,) * (len(extent) - 1 - axis_at))
    return factor_of


def scatter_about(stream_key, shape, width, most, pieces=(), held_as=jnp.bfloat16):
    level = block_scale(stream_key, shape, pieces, -0.22, 0.18) if pieces else 1.0
    drawn = jax.random.normal(stream_key, shape, jnp.float32) * width * level
    return jnp.minimum(jnp.maximum(drawn, -most), most).astype(held_as)


def setup_inputs(seed: int = 0) -> dict:
    key_of = jax.random.split(jax.random.key(seed), 7)
    return {
        "grad_out": scatter_about(key_of[0], (SEQ, D), 1.0, 6.0, ((0, 16), (1, 16))),
        "out_weight": scatter_about(key_of[1], (D, D), D ** -0.5, 0.0625, ((0, 16),)),
        "query_gate": scatter_about(key_of[2], (SEQ, D), 1.0, 6.0, ((0, 16), (1, 16))),
        "key_branch": scatter_about(key_of[3], (SEQ, D), 1.0, 6.0, ((0, 16), (1, 16))),
        "value_branch": scatter_about(key_of[4], (SEQ, D), 1.0, 6.0, ((0, 16), (1, 16))),
        "filter_taps": draw_filter_taps(jax.random.fold_in(key_of[6], 71), 0),
    }


def build_tables(seg_len):
    twice_length = 2 * seg_len
    freq_index = jnp.arange(twice_length, dtype=jnp.int32)
    row_index = jnp.arange(seg_len, dtype=jnp.int32)
    angle_unit = 2.0 * math.pi / twice_length
    fwd_phase = (freq_index[:, None] * row_index[None, :] % twice_length).astype(jnp.float32) * angle_unit
    back_phase = (freq_index[None, :] * (seg_len - row_index[:, None]) % twice_length).astype(jnp.float32) * angle_unit
    window_pos = (freq_index + seg_len) % twice_length
    window_phase = (freq_index[None, :] * window_pos[:, None] % twice_length).astype(jnp.float32) * angle_unit
    parity = jnp.where(freq_index % 2 == 0, 1.0, -1.0).astype(jnp.float32)[:, None]
    return (jnp.cos(fwd_phase).astype(jnp.bfloat16), jnp.sin(fwd_phase).astype(jnp.bfloat16), jnp.cos(back_phase).astype(jnp.bfloat16), jnp.sin(back_phase).astype(jnp.bfloat16), jnp.cos(window_phase).astype(jnp.bfloat16), jnp.sin(window_phase).astype(jnp.bfloat16), parity)

def transform_roundtrip(values):
    rounded = lax.optimization_barrier(values.astype(jnp.bfloat16))
    return rounded.astype(jnp.float32)

def reference(grad_out, out_weight, query_gate, key_branch, value_branch, filter_taps):
    twice_length = 2 * LS
    highest_precision = lax.Precision.HIGHEST
    grad_mix = jnp.dot(grad_out, out_weight.T, preferred_element_type=jnp.float32)
    gated_grad = (grad_mix * query_gate.astype(jnp.float32)).astype(jnp.bfloat16)
    conv_input = (key_branch.astype(jnp.float32) * value_branch.astype(jnp.float32)).astype(jnp.bfloat16)
    cosine_forward, sine_forward, cosine_backward, sine_backward, cosine_window, sine_window, parity = build_tables(LS)

    def spectra(whole):
        block_list = whole.astype(jnp.float32).reshape(N_SEQ, LS, D)
        cosine_piece = jnp.einsum('qk,rkb->rqb', cosine_forward.astype(jnp.float32), block_list, precision=highest_precision)
        sine_piece = jnp.einsum('qk,rkb->rqb', sine_forward.astype(jnp.float32), block_list, precision=highest_precision)
        return (cosine_piece, sine_piece)
    grad_cos, grad_sin = spectra(gated_grad)
    conv_cos, conv_sin = spectra(conv_input)
    tap_cos, tap_sin = spectra(filter_taps)
    kern_cos = jnp.concatenate([jnp.zeros_like(tap_cos[:1]), tap_cos[:-1]], 0) + parity * tap_cos
    kern_sin = jnp.concatenate([jnp.zeros_like(tap_sin[:1]), tap_sin[:-1]], 0) + parity * tap_sin

    def shifted_spec(spec, offset):
        return jnp.concatenate([spec[offset:], jnp.zeros_like(spec[:offset])], 0)
    running_real = jnp.zeros_like(grad_cos)
    running_imaginary = jnp.zeros_like(grad_cos)
    windows = []
    for offset in range(N_SEQ):
        later_cos = shifted_spec(grad_cos, offset)
        later_sin = shifted_spec(grad_sin, offset)
        running_real = running_real + later_cos * kern_cos[offset] + later_sin * kern_sin[offset]
        running_imaginary = running_imaginary + later_sin * kern_cos[offset] - later_cos * kern_sin[offset]
        product_real = transform_roundtrip(conv_cos * later_cos + conv_sin * later_sin)
        product_imaginary = transform_roundtrip(conv_sin * later_cos - conv_cos * later_sin)
        real_total = lax.optimization_barrier(jnp.sum(product_real, axis=0))
        imag_total = lax.optimization_barrier(jnp.sum(product_imaginary, axis=0))
        window = (jnp.dot(cosine_window.astype(jnp.float32), real_total, precision=highest_precision) - jnp.dot(sine_window.astype(jnp.float32), imag_total, precision=highest_precision)) / twice_length
        windows.append(window)
    convolution_gradient = (jnp.einsum('ux,axo->auo', cosine_backward.astype(jnp.float32), transform_roundtrip(running_real), precision=highest_precision) - jnp.einsum('ux,axo->auo', sine_backward.astype(jnp.float32), transform_roundtrip(running_imaginary), precision=highest_precision)) / twice_length
    convolution_gradient = convolution_gradient.reshape(SEQ, D)
    key_grad = (convolution_gradient * value_branch.astype(jnp.float32)).astype(jnp.bfloat16)
    value_grad = (convolution_gradient * key_branch.astype(jnp.float32)).astype(jnp.bfloat16)
    lag_blocks = []
    for offset in range(N_SEQ):
        block_sum = windows[offset][LS:]
        if offset + 1 < N_SEQ:
            block_sum = block_sum + windows[offset + 1][:LS]
        lag_blocks.append(block_sum)
    lag_grad = jnp.concatenate(lag_blocks, 0)
    filter_grad = lag_grad * (1.0 / math.sqrt(SEQ))
    return (key_grad, value_grad, filter_grad)
```

```python
import functools
import math

import jax
import jax.numpy as jnp
import numpy as np
from jax import lax
from jax.experimental import pallas as pl
from jax.experimental.pallas import tpu as pltpu
from jax.sharding import PartitionSpec as P

F32 = jnp.float32
BF16 = jnp.bfloat16
MESH = pl.DeviceIdType.MESH

N_SEQ = 16
N_CH = 16
NZ = 8
LS = 128
CH = 512
SUB = CH // N_SEQ
SEG = 256
NSEG = LS * N_SEQ // SEG


def tables():
    m = 2 * SEG
    t = np.arange(SEG)
    theta = 2.0 * np.pi * ((t[:, None] * t[None, :]) % m) / m
    fwd = np.concatenate([np.cos(theta), np.sin(theta)], 1)
    fwd[:, SEG] = np.where(t % 2 == 0, 1.0, -1.0)
    weight = np.full((m, 1), 2.0 / m)
    weight[0] = weight[SEG] = 1.0 / m
    return jnp.asarray(fwd, BF16), jnp.asarray(weight * fwd.T, BF16)


Z_OFF = (0, -1, -2, -3, 1, 2, 3, 4)
PLUS = (0, 1, 2, 3, 7)
MINUS = (0, 4, 5, 6, 7)
HALF = LS // 2


def kernel(
    go_hbm, w_hbm, q_hbm, key_hbm, val_hbm, taps_hbm, fwd_hbm, inv_hbm,
    kg_ref, vg_ref, fg_ref,
    x_v, w_v, q_v, key_v, val_v, taps_v, fwd_v, inv_v, acc,
    ct_s, tt_s, gt_s, qt, c_r, t_r, g_r, gsp, ksp, csp, abuf, y_s, l_s, y_r, l_r,
    in_sem, w_sem, ring_send, ring_recv, a2a_send, a2a_recv,
):
    s = lax.axis_index("seq")
    c = lax.axis_index("ch")
    z = c // 2
    h = c % 2

    def ch_of(zz, hh):
        return lax.rem(zz + 2 * NZ, NZ) * 2 + hh

    up = ch_of(z + 1, h)
    down = ch_of(z - 1, h)
    across = z * 2 + (1 - h)

    barrier = pltpu.get_barrier_semaphore()
    for peer in (up, down, across):
        pl.semaphore_signal(barrier, inc=1, device_id={"ch": peer}, device_id_type=MESH)
    for k in range(1, N_SEQ):
        pl.semaphore_signal(
            barrier, inc=1, device_id={"seq": lax.rem(s + k, N_SEQ)}, device_id_type=MESH
        )

    loads = []
    for i, (src, dst) in enumerate((
        (key_hbm, key_v), (val_hbm, val_v), (taps_hbm, taps_v), (q_hbm, q_v),
        (go_hbm, x_v.at[0]), (fwd_hbm, fwd_v), (inv_hbm, inv_v),
    )):
        copy = pltpu.make_async_copy(src, dst, in_sem.at[i])
        copy.start()
        loads.append(copy)
    w_loads = []
    for slot in range(N_CH):
        own = slot < NZ
        chunk = ch_of(z + Z_OFF[slot % NZ], h if own else 1 - h)
        copy = pltpu.make_async_copy(
            w_hbm.at[:, pl.ds(pl.multiple_of(chunk * CH, CH), CH)], w_v.at[slot], w_sem.at[slot]
        )
        w_loads.append(copy)
    order = (0, 1, 4, 8, 2, 5, 9, 12, 3, 6, 10, 13, 7, 11, 14, 15)
    for slot in order:
        w_loads[slot].start()

    loads[0].wait()
    loads[1].wait()
    ct_s[...] = (key_v[...].astype(F32) * val_v[...].astype(F32)).T.astype(BF16)
    loads[2].wait()
    tt_s[...] = taps_v[...].astype(F32).T.astype(BF16)
    loads[4].wait()

    pl.semaphore_wait(barrier, 3 + N_SEQ - 1)

    rows = (pl.ds(0, HALF), pl.ds(HALF, HALF))
    sent = []

    def push(src, dst, half, to):
        copy = pltpu.make_async_remote_copy(
            src_ref=x_v.at[src, rows[half]],
            dst_ref=x_v.at[dst, rows[half]],
            send_sem=ring_send.at[len(sent)],
            recv_sem=ring_recv.at[dst, half],
            device_id={"ch": to},
            device_id_type=MESH,
        )
        copy.start()
        sent.append(copy)

    def arrived(slot, half):
        pltpu.make_async_remote_copy(
            src_ref=x_v.at[slot, rows[half]],
            dst_ref=x_v.at[slot, rows[half]],
            send_sem=ring_send.at[0],
            recv_sem=ring_recv.at[slot, half],
            device_id={"ch": up},
            device_id_type=MESH,
        ).wait_recv()

    def mult(slot):
        w_loads[slot].wait()
        part = lax.dot_general(
            w_v[slot], x_v[slot], (((1,), (1,)), ((), ())), preferred_element_type=F32
        )
        if slot == 0:
            acc[...] = part
        else:
            acc[...] += part

    def forward(step, base):
        if step < 4:
            for chain, to, last in ((PLUS, up, 0), (MINUS, down, 1)):
                for half in (0, 1):
                    arrived(base + chain[step], half)
                    if step < 3 or half == last:
                        push(base + chain[step], base + chain[step + 1], half, to)
        else:
            arrived(base + PLUS[4], 0)
            arrived(base + PLUS[4], 1)

    for half in (0, 1):
        push(0, PLUS[1], half, up)
        push(0, MINUS[1], half, down)
    for half in (0, 1):
        push(0, NZ, half, across)

    def scatter(block, recv, which):
        my_row = pl.ds(pl.multiple_of((s // 2) * SUB, SUB), SUB)
        my_col = pl.ds(pl.multiple_of((s % 2) * LS, LS), LS)
        pltpu.make_async_copy(
            block.at[pl.ds(pl.multiple_of(s * SUB, SUB), SUB)],
            recv.at[my_row, my_col],
            a2a_recv.at[which],
        ).start()
        for k in range(1, N_SEQ):
            to = lax.rem(s + k, N_SEQ)
            pltpu.make_async_remote_copy(
                src_ref=block.at[pl.ds(pl.multiple_of(to * SUB, SUB), SUB)],
                dst_ref=recv.at[my_row, my_col],
                send_sem=a2a_send.at[which],
                recv_sem=a2a_recv.at[which],
                device_id={"seq": to},
                device_id_type=MESH,
            ).start()

    def collect(block, recv, which):
        my_row = pl.ds(pl.multiple_of(s * SUB, SUB), SUB)

        def piece(i):
            return block.at[
                pl.ds(pl.multiple_of((i // 2) * SUB, SUB), SUB),
                pl.ds(pl.multiple_of((i % 2) * LS, LS), LS),
            ]

        pltpu.make_async_copy(piece(s), recv.at[my_row], a2a_recv.at[which]).start()
        for k in range(1, N_SEQ):
            to = lax.rem(s + k, N_SEQ)
            pltpu.make_async_remote_copy(
                src_ref=piece(to),
                dst_ref=recv.at[my_row],
                send_sem=a2a_send.at[which],
                recv_sem=a2a_recv.at[which],
                device_id={"seq": to},
                device_id_type=MESH,
            ).start()

    def all_in(recv, which):
        pltpu.make_async_copy(recv, recv, a2a_recv.at[which]).wait()

    def all_out(block, which):
        rows_sent = block.shape[0] - block.shape[0] // N_SEQ
        part = block.at[pl.ds(0, rows_sent)]
        pltpu.make_async_copy(part, part, a2a_send.at[which]).wait()

    scatter(ct_s, c_r, 0)
    scatter(tt_s, t_r, 1)

    loads[3].wait()
    qt[...] = q_v[...].astype(F32).T
    mult(0)

    sign = jnp.where(
        lax.broadcasted_iota(jnp.int32, (1, SEG), 1) % 2 == 0, 1.0, -1.0
    ).astype(F32)
    first = lax.broadcasted_iota(jnp.int32, (1, SEG), 1) == 0

    forward(1, 0)
    mult(1)
    mult(4)
    for half in (0, 1):
        arrived(NZ, half)
        push(NZ, NZ + PLUS[1], half, up)
        push(NZ, NZ + MINUS[1], half, down)
    mult(8)
    forward(2, 0)
    mult(2)
    mult(5)
    forward(1, NZ)
    mult(9)
    mult(12)
    forward(3, 0)

    def put3(ref, cos, sin):
        ref[:, pl.ds(0, SEG)] = cos
        ref[:, pl.ds(SEG, SEG)] = jnp.where(first, 0.0, sin)
        ref[:, pl.ds(2 * SEG, SEG)] = jnp.where(first, sin, cos)

    loads[5].wait()
    all_in(c_r, 0)
    spec = jnp.dot(c_r[...], fwd_v[...], preferred_element_type=F32)
    put3(csp, spec[:, :SEG], spec[:, SEG:])
    mult(3)
    mult(6)
    forward(2, NZ)
    all_in(t_r, 1)
    spec = jnp.dot(t_r[...], fwd_v[...], preferred_element_type=F32)
    before = jnp.concatenate([jnp.zeros((SUB, 2 * SEG), F32), spec[:-SUB]], 0)
    put3(
        ksp,
        spec[:, :SEG] + sign * before[:, :SEG],
        spec[:, SEG:] + sign * before[:, SEG:],
    )
    mult(10)
    mult(13)
    forward(4, 0)
    mult(7)
    forward(3, NZ)
    mult(11)
    mult(14)
    loads[6].wait()
    forward(4, NZ)
    mult(15)

    gt_s[...] = (acc[...] * qt[...]).astype(BF16)
    scatter(gt_s, g_r, 2)
    all_in(g_r, 2)
    gsp[...] = jnp.dot(g_r[...], fwd_v[...], preferred_element_type=F32)

    tile = 16
    cols = SEG // 128

    def at(ref, seg, row, part, col):
        return ref[
            pl.ds(pl.multiple_of(seg * SUB + row * tile, tile), tile),
            pl.ds(pl.multiple_of(part * SEG + col * 128, 128), 128),
        ]

    def put(seg, row, part, col, value):
        abuf[
            pl.ds(pl.multiple_of(seg * SUB + row * tile, tile), tile),
            pl.ds(pl.multiple_of(part * SEG + col * 128, 128), 128),
        ] = value.astype(BF16)

    def pair(ref, i, r, row, col):
        ga, gb = at(gsp, i, row, 0, col), at(gsp, i, row, 1, col)
        ka, kb, k2 = (at(ref, r, row, part, col) for part in range(3))
        return ga * ka + gb * kb, gb * k2 - ga * kb

    @pl.loop(0, (SUB // tile) * cols)
    def _(pos):
        row, col = pos // cols, pos % cols
        for j in range(NSEG):
            re = im = None
            for i in range(j, NSEG):
                a, b = pair(ksp, i, i - j, row, col)
                re, im = (a, b) if re is None else (re + a, im + b)
            put(j, row, 0, col, re)
            put(j, row, 1, col, im)

    y_s[...] = jnp.dot(abuf[...], inv_v[...], preferred_element_type=F32).astype(BF16)
    collect(y_s, y_r, 3)

    lane_sign = sign[:, :128]

    @pl.loop(0, (SUB // tile) * cols)
    def _(pos):
        row, col = pos // cols, pos % cols
        later = None
        for r in reversed(range(NSEG)):
            re = im = None
            for j in range(NSEG - r):
                a, b = pair(csp, j + r, j, row, col)
                re, im = (a, b) if re is None else (re + a, im + b)
            if later is None:
                put(r, row, 0, col, re)
                put(r, row, 1, col, im)
            else:
                put(r, row, 0, col, re + lane_sign * later[0])
                put(r, row, 1, col, im + lane_sign * later[1])
            later = (re, im)

    l_s[...] = jnp.dot(abuf[...], inv_v[...], preferred_element_type=F32).astype(BF16)
    collect(l_s, l_r, 4)

    all_in(y_r, 3)
    conv = y_r[...].astype(F32).T
    kg_ref[...] = (conv * val_v[...].astype(F32)).astype(BF16)
    vg_ref[...] = (conv * key_v[...].astype(F32)).astype(BF16)
    all_in(l_r, 4)
    fg_ref[...] = l_r[...].astype(F32).T * (1.0 / math.sqrt(LS * N_SEQ))

    for copy in sent:
        copy.wait_send()
    for which, block in enumerate((ct_s, tt_s, gt_s, y_s, l_s)):
        all_out(block, which)


def shards(grad_out, out_weight, query_gate, key_branch, value_branch, filter_taps):
    fwd, inv = tables()
    any_spec = pl.BlockSpec(memory_space=pl.ANY)
    vmem_spec = pl.BlockSpec(memory_space=pltpu.VMEM)
    block = (LS, CH)
    turned = (CH, LS)
    local = (NSEG * SUB, SEG)
    return pl.pallas_call(
        kernel,
        out_shape=(
            jax.ShapeDtypeStruct(block, BF16),
            jax.ShapeDtypeStruct(block, BF16),
            jax.ShapeDtypeStruct(block, F32),
        ),
        in_specs=[any_spec] * 8,
        out_specs=(vmem_spec,) * 3,
        scratch_shapes=[
            pltpu.VMEM((N_CH, LS, CH), BF16),
            pltpu.VMEM((N_CH, CH, CH), BF16),
            pltpu.VMEM(block, BF16),
            pltpu.VMEM(block, BF16),
            pltpu.VMEM(block, BF16),
            pltpu.VMEM(block, BF16),
            pltpu.VMEM((SEG, 2 * SEG), BF16),
            pltpu.VMEM((2 * SEG, SEG), BF16),
            pltpu.VMEM(turned, F32),
            pltpu.VMEM(turned, BF16),
            pltpu.VMEM(turned, BF16),
            pltpu.VMEM(turned, BF16),
            pltpu.VMEM(turned, F32),
            pltpu.VMEM(local, BF16),
            pltpu.VMEM(local, BF16),
            pltpu.VMEM(local, BF16),
            pltpu.VMEM((NSEG * SUB, 2 * SEG), F32),
            pltpu.VMEM((NSEG * SUB, 3 * SEG), F32),
            pltpu.VMEM((NSEG * SUB, 3 * SEG), F32),
            pltpu.VMEM((NSEG * SUB, 2 * SEG), BF16),
            pltpu.VMEM(local, BF16),
            pltpu.VMEM(local, BF16),
            pltpu.VMEM(turned, BF16),
            pltpu.VMEM(turned, BF16),
            pltpu.SemaphoreType.DMA((7,)),
            pltpu.SemaphoreType.DMA((N_CH,)),
            pltpu.SemaphoreType.DMA((30,)),
            pltpu.SemaphoreType.DMA((N_CH, 2)),
            pltpu.SemaphoreType.DMA((5,)),
            pltpu.SemaphoreType.DMA((5,)),
        ],
        compiler_params=pltpu.CompilerParams(
            collective_id=0, has_side_effects=True, vmem_limit_bytes=40 << 20
        ),
        name="hyena_backward",
    )(grad_out, out_weight, query_gate, key_branch, value_branch, filter_taps, fwd, inv)


def solution(mesh):
    spec = P("seq", "ch")
    return jax.shard_map(
        shards,
        mesh=mesh,
        in_specs=(spec, P("ch", None), spec, spec, spec, spec),
        out_specs=(spec, spec, spec),
        check_vma=False,
    )
```

```python
import functools
import math

import jax
import jax.numpy as jnp
import numpy as np
from jax import lax
from jax.experimental import pallas as pl
from jax.experimental.pallas import tpu as pltpu
from jax.sharding import PartitionSpec as P

F32 = jnp.float32
BF16 = jnp.bfloat16
MESH = pl.DeviceIdType.MESH

VMEM_GRANT = 66060288
N_SEQ = 16
N_CH = 16
NZ = 8
LS = 128
CH = 512
SUB = CH // N_SEQ
SEG = 256
NSEG = LS * N_SEQ // SEG


def tables():
    m = 2 * SEG
    t = np.arange(SEG)
    theta = 2.0 * np.pi * ((t[:, None] * t[None, :]) % m) / m
    fwd = np.concatenate([np.cos(theta), np.sin(theta)], 1)
    fwd[:, SEG] = np.where(t % 2 == 0, 1.0, -1.0)
    weight = np.full((m, 1), 2.0 / m)
    weight[0] = weight[SEG] = 1.0 / m
    return jnp.asarray(fwd, BF16), jnp.asarray(weight * fwd.T, BF16)


Z_OFF = (0, -1, -2, -3, 1, 2, 3, 4)
PLUS = (0, 1, 2, 3, 7)
MINUS = (0, 4, 5, 6, 7)
QUARTER = LS // 4
A, B = (0, 2 * QUARTER), (2 * QUARTER, 2 * QUARTER)
A0, A1, B0, B1 = ((i * QUARTER, QUARTER) for i in range(4))
PARTS = (A, B, A0, A1, B0, B1)


def kernel(
    go_hbm, w_hbm, q_hbm, key_hbm, val_hbm, taps_hbm, fwd_hbm, inv_hbm,
    out_ref,
    x_v, w_v, q_v, key_v, val_v, taps_v, fwd_v, inv_v, acc,
    ct_s, tt_s, gt_s, qt, c_r, t_r, g_r, gsp, ksp, csp, abuf, y_s, l_s, y_r, l_r,
    in_sem, w_sem, ring_send, ring_recv, a2a_send, a2a_recv,
):
    s = lax.axis_index("seq")
    c = lax.axis_index("ch")
    z = c // 2
    h = c % 2

    def ch_of(zz, hh):
        return lax.rem(zz + 2 * NZ, NZ) * 2 + hh

    up = ch_of(z + 1, h)
    down = ch_of(z - 1, h)
    across = z * 2 + (1 - h)

    barrier = pltpu.get_barrier_semaphore()
    for peer in (up, down, across):
        pl.semaphore_signal(barrier, inc=1, device_id={"ch": peer}, device_id_type=MESH)
    for k in range(1, N_SEQ):
        pl.semaphore_signal(
            barrier, inc=1, device_id={"seq": lax.rem(s + k, N_SEQ)}, device_id_type=MESH
        )

    loads = []
    for i, (src, dst) in enumerate((
        (key_hbm, key_v), (val_hbm, val_v), (taps_hbm, taps_v), (q_hbm, q_v),
        (go_hbm, x_v.at[0]), (fwd_hbm, fwd_v), (inv_hbm, inv_v),
    )):
        copy = pltpu.make_async_copy(src, dst, in_sem.at[i])
        copy.start()
        loads.append(copy)
    w_loads = []
    for slot in range(N_CH):
        own = slot < NZ
        chunk = ch_of(z + Z_OFF[slot % NZ], h if own else 1 - h)
        copy = pltpu.make_async_copy(
            w_hbm.at[:, pl.ds(pl.multiple_of(chunk * CH, CH), CH)], w_v.at[slot], w_sem.at[slot]
        )
        w_loads.append(copy)
    order = (0, 1, 4, 8, 2, 5, 9, 12, 3, 6, 10, 13, 7, 11, 14, 15)
    for slot in order:
        w_loads[slot].start()

    loads[0].wait()
    loads[1].wait()
    ct_s[...] = (key_v[...].astype(F32) * val_v[...].astype(F32)).T.astype(BF16)
    loads[2].wait()
    tt_s[...] = taps_v[...].astype(F32).T.astype(BF16)
    loads[4].wait()

    pl.semaphore_wait(barrier, 3 + N_SEQ - 1)

    sent = []

    def push(src, dst, part, to):
        copy = pltpu.make_async_remote_copy(
            src_ref=x_v.at[src, pl.ds(*part)],
            dst_ref=x_v.at[dst, pl.ds(*part)],
            send_sem=ring_send.at[len(sent)],
            recv_sem=ring_recv.at[dst, PARTS.index(part)],
            device_id={"ch": to},
            device_id_type=MESH,
        )
        copy.start()
        sent.append(copy)

    def arrived(slot, part):
        pltpu.make_async_remote_copy(
            src_ref=x_v.at[slot, pl.ds(*part)],
            dst_ref=x_v.at[slot, pl.ds(*part)],
            send_sem=ring_send.at[0],
            recv_sem=ring_recv.at[slot, PARTS.index(part)],
            device_id={"ch": up},
            device_id_type=MESH,
        ).wait_recv()

    def mult(slot):
        w_loads[slot].wait()
        part = lax.dot_general(
            w_v[slot], x_v[slot], (((1,), (1,)), ((), ())), preferred_element_type=F32
        )
        if slot == 0:
            acc[...] = part
        else:
            acc[...] += part

    def ring(step, base, whole, quarters, cross=False):
        for chain, to, last in ((PLUS, up, quarters[0]), (MINUS, down, quarters[1])):
            part = whole if step < 4 else last
            arrived(base + chain[step], part)
            if step < 3:
                push(base + chain[step], base + chain[step + 1], part, to)
            elif step == 3:
                push(base + chain[step], base + chain[step + 1], last, to)
            if cross:
                push(base + chain[step], NZ + chain[step], part, across)

    def start_ring(base, part):
        push(base, base + PLUS[1], part, up)
        push(base, base + MINUS[1], part, down)

    ring_a = functools.partial(ring, base=0, whole=A, quarters=(A0, A1), cross=True)
    ring_b = functools.partial(ring, base=0, whole=B, quarters=(B0, B1))
    ring_p = functools.partial(ring, base=NZ, whole=B, quarters=(B0, B1))

    start_ring(0, A)
    push(0, NZ, B, across)
    push(0, NZ, A, across)
    start_ring(0, B)

    def scatter(block, recv, which):
        my_row = pl.ds(pl.multiple_of((s // 2) * SUB, SUB), SUB)
        my_col = pl.ds(pl.multiple_of((s % 2) * LS, LS), LS)
        pltpu.make_async_copy(
            block.at[pl.ds(pl.multiple_of(s * SUB, SUB), SUB)],
            recv.at[my_row, my_col],
            a2a_recv.at[which],
        ).start()
        for k in range(1, N_SEQ):
            to = lax.rem(s + k, N_SEQ)
            pltpu.make_async_remote_copy(
                src_ref=block.at[pl.ds(pl.multiple_of(to * SUB, SUB), SUB)],
                dst_ref=recv.at[my_row, my_col],
                send_sem=a2a_send.at[which],
                recv_sem=a2a_recv.at[which],
                device_id={"seq": to},
                device_id_type=MESH,
            ).start()

    def collect(block, recv, which):
        my_row = pl.ds(pl.multiple_of(s * SUB, SUB), SUB)

        def piece(i):
            return block.at[
                pl.ds(pl.multiple_of((i // 2) * SUB, SUB), SUB),
                pl.ds(pl.multiple_of((i % 2) * LS, LS), LS),
            ]

        pltpu.make_async_copy(piece(s), recv.at[my_row], a2a_recv.at[which]).start()
        for k in range(1, N_SEQ):
            to = lax.rem(s + k, N_SEQ)
            pltpu.make_async_remote_copy(
                src_ref=piece(to),
                dst_ref=recv.at[my_row],
                send_sem=a2a_send.at[which],
                recv_sem=a2a_recv.at[which],
                device_id={"seq": to},
                device_id_type=MESH,
            ).start()

    def all_in(recv, which):
        pltpu.make_async_copy(recv, recv, a2a_recv.at[which]).wait()

    def all_out(block, which):
        rows_sent = block.shape[0] - block.shape[0] // N_SEQ
        part = block.at[pl.ds(0, rows_sent)]
        pltpu.make_async_copy(part, part, a2a_send.at[which]).wait()

    scatter(ct_s, c_r, 0)
    scatter(tt_s, t_r, 1)

    loads[3].wait()
    qt[...] = q_v[...].astype(F32).T
    mult(0)

    sign = jnp.where(
        lax.broadcasted_iota(jnp.int32, (1, SEG), 1) % 2 == 0, 1.0, -1.0
    ).astype(F32)
    first = lax.broadcasted_iota(jnp.int32, (1, SEG), 1) == 0

    ring_a(1)
    ring_b(1)
    mult(1)
    mult(4)
    arrived(NZ, B)
    start_ring(NZ, B)
    arrived(NZ, A)
    mult(8)
    ring_a(2)
    ring_b(2)
    mult(2)
    mult(5)
    ring_p(1)
    ring_a(3)
    ring_b(3)

    def put3(ref, cos, sin):
        ref[:, pl.ds(0, SEG)] = cos
        ref[:, pl.ds(SEG, SEG)] = jnp.where(first, 0.0, sin)
        ref[:, pl.ds(2 * SEG, SEG)] = jnp.where(first, sin, cos)

    loads[5].wait()
    all_in(c_r, 0)
    spec = jnp.dot(c_r[...], fwd_v[...], preferred_element_type=F32)
    put3(csp, spec[:, :SEG], spec[:, SEG:])
    mult(3)
    ring_p(2)
    mult(6)
    ring_a(4)
    all_in(t_r, 1)
    spec = jnp.dot(t_r[...], fwd_v[...], preferred_element_type=F32)
    before = jnp.concatenate([jnp.zeros((SUB, 2 * SEG), F32), spec[:-SUB]], 0)
    put3(
        ksp,
        spec[:, :SEG] + sign * before[:, :SEG],
        spec[:, SEG:] + sign * before[:, SEG:],
    )
    loads[6].wait()
    ring_b(4)
    mult(7)
    ring_p(3)
    for slot in (9, 12, 10, 13):
        arrived(slot, A)
        mult(slot)
    for slot in (11, 14):
        arrived(slot, A)
        mult(slot)
    ring_p(4)
    arrived(15, A0)
    arrived(15, A1)
    mult(15)

    gt_s[...] = (acc[...] * qt[...]).astype(BF16)
    scatter(gt_s, g_r, 2)
    all_in(g_r, 2)
    gsp[...] = jnp.dot(g_r[...], fwd_v[...], preferred_element_type=F32)

    tile = 16
    cols = SEG // 128

    def at(ref, seg, row, part, col):
        return ref[
            pl.ds(pl.multiple_of(seg * SUB + row * tile, tile), tile),
            pl.ds(pl.multiple_of(part * SEG + col * 128, 128), 128),
        ]

    def put(seg, row, part, col, value):
        abuf[
            pl.ds(pl.multiple_of(seg * SUB + row * tile, tile), tile),
            pl.ds(pl.multiple_of(part * SEG + col * 128, 128), 128),
        ] = value.astype(BF16)

    def pair(ref, i, r, row, col):
        ga, gb = at(gsp, i, row, 0, col), at(gsp, i, row, 1, col)
        ka, kb, k2 = (at(ref, r, row, part, col) for part in range(3))
        return ga * ka + gb * kb, gb * k2 - ga * kb

    @pl.loop(0, (SUB // tile) * cols)
    def _(pos):
        row, col = pos // cols, pos % cols
        for j in range(NSEG):
            re = im = None
            for i in range(j, NSEG):
                a, b = pair(ksp, i, i - j, row, col)
                re, im = (a, b) if re is None else (re + a, im + b)
            put(j, row, 0, col, re)
            put(j, row, 1, col, im)

    y_s[...] = jnp.dot(abuf[...], inv_v[...], preferred_element_type=F32).astype(BF16)
    collect(y_s, y_r, 3)

    lane_sign = sign[:, :128]

    @pl.loop(0, (SUB // tile) * cols)
    def _(pos):
        row, col = pos // cols, pos % cols
        later = None
        for r in reversed(range(NSEG)):
            re = im = None
            for j in range(NSEG - r):
                a, b = pair(csp, j + r, j, row, col)
                re, im = (a, b) if re is None else (re + a, im + b)
            if later is None:
                put(r, row, 0, col, re)
                put(r, row, 1, col, im)
            else:
                put(r, row, 0, col, re + lane_sign * later[0])
                put(r, row, 1, col, im + lane_sign * later[1])
            later = (re, im)

    l_s[...] = jnp.dot(abuf[...], inv_v[...], preferred_element_type=F32).astype(BF16)
    collect(l_s, l_r, 4)

    all_in(y_r, 3)
    out_ref[pl.ds(0, LS)] = y_r[...].astype(F32).T.astype(BF16)
    all_in(l_r, 4)
    out_ref[pl.ds(LS, LS)] = l_r[...].astype(F32).T.astype(BF16)

    for copy in sent:
        copy.wait_send()
    for which, block in enumerate((ct_s, tt_s, gt_s, y_s, l_s)):
        all_out(block, which)


def shards(grad_out, out_weight, query_gate, key_branch, value_branch, filter_taps):
    fwd, inv = tables()
    any_spec = pl.BlockSpec(memory_space=pl.ANY)
    vmem_spec = pl.BlockSpec(memory_space=pltpu.VMEM)
    block = (LS, CH)
    turned = (CH, LS)
    local = (NSEG * SUB, SEG)
    both = pl.pallas_call(
        kernel,
        out_shape=jax.ShapeDtypeStruct((2 * LS, CH), BF16),
        in_specs=[any_spec] * 8,
        out_specs=vmem_spec,
        scratch_shapes=[
            pltpu.VMEM((N_CH, LS, CH), BF16),
            pltpu.VMEM((N_CH, CH, CH), BF16),
            pltpu.VMEM(block, BF16),
            pltpu.VMEM(block, BF16),
            pltpu.VMEM(block, BF16),
            pltpu.VMEM(block, BF16),
            pltpu.VMEM((SEG, 2 * SEG), BF16),
            pltpu.VMEM((2 * SEG, SEG), BF16),
            pltpu.VMEM(turned, F32),
            pltpu.VMEM(turned, BF16),
            pltpu.VMEM(turned, BF16),
            pltpu.VMEM(turned, BF16),
            pltpu.VMEM(turned, F32),
            pltpu.VMEM(local, BF16),
            pltpu.VMEM(local, BF16),
            pltpu.VMEM(local, BF16),
            pltpu.VMEM((NSEG * SUB, 2 * SEG), F32),
            pltpu.VMEM((NSEG * SUB, 3 * SEG), F32),
            pltpu.VMEM((NSEG * SUB, 3 * SEG), F32),
            pltpu.VMEM((NSEG * SUB, 2 * SEG), BF16),
            pltpu.VMEM(local, BF16),
            pltpu.VMEM(local, BF16),
            pltpu.VMEM(turned, BF16),
            pltpu.VMEM(turned, BF16),
            pltpu.SemaphoreType.DMA((7,)),
            pltpu.SemaphoreType.DMA((N_CH,)),
            pltpu.SemaphoreType.DMA((34,)),
            pltpu.SemaphoreType.DMA((N_CH, 6)),
            pltpu.SemaphoreType.DMA((5,)),
            pltpu.SemaphoreType.DMA((5,)),
        ],
        compiler_params=pltpu.CompilerParams(
            collective_id=0, has_side_effects=True, vmem_limit_bytes=VMEM_GRANT
        ),
        name="hyena_backward",
    )(grad_out, out_weight, query_gate, key_branch, value_branch, filter_taps, fwd, inv)
    conv = both[:LS].astype(F32)
    lag = both[LS:].astype(F32)
    return (
        (conv * value_branch.astype(F32)).astype(BF16),
        (conv * key_branch.astype(F32)).astype(BF16),
        lag * (1.0 / math.sqrt(LS * N_SEQ)),
    )


def solution(mesh):
    spec = P("seq", "ch")
    return jax.shard_map(
        shards,
        mesh=mesh,
        in_specs=(spec, P("ch", None), spec, spec, spec, spec),
        out_specs=(spec, spec, spec),
        check_vma=False,
    )
```

```python
import functools
import math

import jax
import jax.numpy as jnp
import numpy as np
from jax import lax
from jax.experimental import pallas as pl
from jax.experimental.pallas import tpu as pltpu
from jax.sharding import PartitionSpec as P

F32 = jnp.float32
BF16 = jnp.bfloat16
MESH = pl.DeviceIdType.MESH

VMEM_GRANT = 66060288
N_SEQ = 16
N_CH = 16
NZ = 8
LS = 128
CH = 512
SUB = CH // N_SEQ
SEG = 256
NSEG = LS * N_SEQ // SEG


def tables():
    m = 2 * SEG
    t = np.arange(SEG)
    theta = 2.0 * np.pi * ((t[:, None] * t[None, :]) % m) / m
    fwd = np.concatenate([np.cos(theta), np.sin(theta)], 1)
    fwd[:, SEG] = np.where(t % 2 == 0, 1.0, -1.0)
    weight = np.full((m, 1), 2.0 / m)
    weight[0] = weight[SEG] = 1.0 / m
    return jnp.asarray(fwd, BF16), jnp.asarray(weight * fwd.T, BF16)


Z_OFF = (0, -1, -2, -3, 1, 2, 3, 4)
PLUS = (0, 1, 2, 3, 7)
MINUS = (0, 4, 5, 6, 7)
CHUNK = LS // 4
ROWS_A = (0, CHUNK)
ROWS_B = (2 * CHUNK, 3 * CHUNK)
RING_RECV = 50
HOPS = tuple(
    (dx, dy, dc) for dx in (2, 1, 3, 0) for dy in (1, 0) for dc in (0, 1) if dx or dy or dc
)


def kernel(
    go_hbm, w_hbm, q_hbm, key_hbm, val_hbm, taps_hbm, fwd_hbm, inv_hbm,
    out_ref,
    x_v, w_v, in_v, fwd_v, inv_v, acc,
    ct_s, tt_s, gt_s, qt, c_r, t_r, g_r, gsp, ksp, csp, abuf, y_s, l_s, y_r, l_r,
    in_sem, w_sem, ring_send, ring_recv, a2a_send, a2a_recv,
):
    s = lax.axis_index("seq")
    c = lax.axis_index("ch")
    z = c // 2
    h = c % 2

    def ch_of(zz, hh):
        return lax.rem(zz + 2 * NZ, NZ) * 2 + hh

    up = ch_of(z + 1, h)
    down = ch_of(z - 1, h)
    across = z * 2 + (1 - h)

    barrier = pltpu.get_barrier_semaphore()
    for peer in (up, down, across):
        pl.semaphore_signal(barrier, inc=1, device_id={"ch": peer}, device_id_type=MESH)
    def seq_of(hop):
        dx, dy, dc = hop
        return (
            lax.rem(s // 4 + dx, 4) * 4
            + lax.rem((s // 2) % 2 + dy, 2) * 2
            + lax.rem(s % 2 + dc, 2)
        )

    for hop in HOPS:
        pl.semaphore_signal(
            barrier, inc=1, device_id={"seq": seq_of(hop)}, device_id_type=MESH
        )

    own = pltpu.make_async_copy(go_hbm, x_v.at[0], in_sem.at[0])
    own.start()
    for i, src in enumerate((key_hbm, val_hbm, taps_hbm, q_hbm)):
        pltpu.make_async_copy(src, in_v.at[i], in_sem.at[1]).start()
    for slot in range(N_CH):
        chunk = ch_of(z + Z_OFF[slot % NZ], h if slot < NZ else 1 - h)
        pltpu.make_async_copy(
            w_hbm.at[:, pl.ds(pl.multiple_of(chunk * CH, CH), CH)], w_v.at[slot], w_sem
        ).start()
    fwd_load = pltpu.make_async_copy(fwd_hbm, fwd_v, in_sem.at[2])
    fwd_load.start()
    inv_load = pltpu.make_async_copy(inv_hbm, inv_v, in_sem.at[3])
    inv_load.start()

    own.wait()
    pl.semaphore_wait(barrier, 3 + N_SEQ - 1)

    keys = {}

    def recv_sem(key):
        return ring_recv.at[keys.setdefault(key, len(keys))]

    def key_of(slot, row):
        if slot % NZ == 7 and row in ROWS_B:
            return slot
        return slot, row

    def push(src, dst, row, to, key=None):
        pltpu.make_async_remote_copy(
            src_ref=x_v.at[src, pl.ds(row, CHUNK)],
            dst_ref=x_v.at[dst, pl.ds(row, CHUNK)],
            send_sem=ring_send,
            recv_sem=recv_sem(key or key_of(dst, row)),
            device_id={"ch": to},
            device_id_type=MESH,
        ).start()

    def arrived(slot, row, rows=CHUNK, key=None):
        part = x_v.at[slot, pl.ds(row, rows)]
        pltpu.make_async_copy(part, part, recv_sem(key or key_of(slot, row))).wait()

    def arrived_across(slot):
        arrived(slot, 0, 2 * CHUNK, ("across", slot))

    def mult(slot):
        part = lax.dot_general(
            w_v[slot], x_v[slot], (((1,), (1,)), ((), ())), preferred_element_type=F32
        )
        if slot == 0:
            acc[...] = part
        else:
            acc[...] += part

    def ring(step, base, rows, cross=False):
        for i, row in enumerate(rows):
            for side, (chain, to) in enumerate(((PLUS, up), (MINUS, down))):
                if step == 4 and (i != side or not cross):
                    continue
                arrived(base + chain[step], row)
                if step < 3 or (step == 3 and i == side):
                    push(base + chain[step], base + chain[step + 1], row, to)
                if cross:
                    slot = NZ + chain[step]
                    push(base + chain[step], slot, row, across, ("across", slot))
        if step == 4 and not cross:
            arrived(base + 7, rows[0], 2 * CHUNK)

    def start_ring(base, row):
        push(base, base + PLUS[1], row, up)
        push(base, base + MINUS[1], row, down)

    ring_a = functools.partial(ring, base=0, rows=ROWS_A, cross=True)
    ring_b = functools.partial(ring, base=0, rows=ROWS_B)
    ring_p = functools.partial(ring, base=NZ, rows=ROWS_B)

    for row in ROWS_A:
        start_ring(0, row)
    for row in ROWS_B:
        push(0, NZ, row, across)
    for row in ROWS_A:
        push(0, NZ, row, across, ("across", NZ))
    for row in ROWS_B:
        start_ring(0, row)

    def scatter(block, recv, which):
        my_row = pl.ds(pl.multiple_of((s // 2) * SUB, SUB), SUB)
        my_col = pl.ds(pl.multiple_of((s % 2) * LS, LS), LS)
        pltpu.make_async_copy(
            block.at[pl.ds(pl.multiple_of(s * SUB, SUB), SUB)],
            recv.at[my_row, my_col],
            a2a_recv.at[which],
        ).start()
        for hop in HOPS:
            to = seq_of(hop)
            pltpu.make_async_remote_copy(
                src_ref=block.at[pl.ds(pl.multiple_of(to * SUB, SUB), SUB)],
                dst_ref=recv.at[my_row, my_col],
                send_sem=a2a_send.at[which],
                recv_sem=a2a_recv.at[which],
                device_id={"seq": to},
                device_id_type=MESH,
            ).start()

    def collect(block, recv, which):
        my_row = pl.ds(pl.multiple_of(s * SUB, SUB), SUB)

        def piece(i):
            return block.at[
                pl.ds(pl.multiple_of((i // 2) * SUB, SUB), SUB),
                pl.ds(pl.multiple_of((i % 2) * LS, LS), LS),
            ]

        pltpu.make_async_copy(piece(s), recv.at[my_row], a2a_recv.at[which]).start()
        for hop in HOPS:
            to = seq_of(hop)
            pltpu.make_async_remote_copy(
                src_ref=piece(to),
                dst_ref=recv.at[my_row],
                send_sem=a2a_send.at[which],
                recv_sem=a2a_recv.at[which],
                device_id={"seq": to},
                device_id_type=MESH,
            ).start()

    def all_in(recv, which):
        pltpu.make_async_copy(recv, recv, a2a_recv.at[which]).wait()

    def all_out(block, which):
        rows_sent = block.shape[0] - block.shape[0] // N_SEQ
        part = block.at[pl.ds(0, rows_sent)]
        pltpu.make_async_copy(part, part, a2a_send.at[which]).wait()

    pltpu.make_async_copy(in_v, in_v, in_sem.at[1]).wait()
    ct_s[...] = (in_v[0].astype(F32) * in_v[1].astype(F32)).T.astype(BF16)
    scatter(ct_s, c_r, 0)
    tt_s[...] = in_v[2].astype(F32).T.astype(BF16)
    scatter(tt_s, t_r, 1)
    qt[...] = in_v[3].astype(F32).T

    sign = jnp.where(
        lax.broadcasted_iota(jnp.int32, (1, SEG), 1) % 2 == 0, 1.0, -1.0
    ).astype(F32)
    first = lax.broadcasted_iota(jnp.int32, (1, SEG), 1) == 0

    ring_a(1)
    ring_b(1)
    for row in ROWS_B:
        arrived(NZ, row)
        start_ring(NZ, row)
    pltpu.make_async_copy(w_v, w_v, w_sem).wait()
    mult(0)
    mult(1)
    mult(4)
    ring_a(2)
    ring_b(2)
    ring_p(1)
    mult(2)
    mult(5)
    arrived_across(NZ)
    mult(8)
    ring_a(3)
    ring_b(3)
    ring_p(2)

    def put3(ref, cos, sin):
        ref[:, pl.ds(0, SEG)] = cos
        ref[:, pl.ds(SEG, SEG)] = jnp.where(first, 0.0, sin)
        ref[:, pl.ds(2 * SEG, SEG)] = jnp.where(first, sin, cos)

    fwd_load.wait()
    all_in(c_r, 0)
    spec = jnp.dot(c_r[...], fwd_v[...], preferred_element_type=F32)
    put3(csp, spec[:, :SEG], spec[:, SEG:])
    mult(3)
    mult(6)
    ring_a(4)
    ring_b(4)
    ring_p(3)
    all_in(t_r, 1)
    spec = jnp.dot(t_r[...], fwd_v[...], preferred_element_type=F32)
    before = jnp.concatenate([jnp.zeros((SUB, 2 * SEG), F32), spec[:-SUB]], 0)
    put3(
        ksp,
        spec[:, :SEG] + sign * before[:, :SEG],
        spec[:, SEG:] + sign * before[:, SEG:],
    )
    inv_load.wait()
    mult(7)
    for slot in (9, 12, 10, 13):
        arrived_across(slot)
        mult(slot)
    ring_p(4)
    for slot in (11, 14, 15):
        arrived_across(slot)
        mult(slot)

    gt_s[...] = (acc[...] * qt[...]).astype(BF16)
    scatter(gt_s, g_r, 2)
    all_in(g_r, 2)
    gsp[...] = jnp.dot(g_r[...], fwd_v[...], preferred_element_type=F32)

    tile = 16
    cols = SEG // 128

    def at(ref, seg, row, part, col):
        return ref[
            pl.ds(pl.multiple_of(seg * SUB + row * tile, tile), tile),
            pl.ds(pl.multiple_of(part * SEG + col * 128, 128), 128),
        ]

    def put(seg, row, part, col, value):
        abuf[
            pl.ds(pl.multiple_of(seg * SUB + row * tile, tile), tile),
            pl.ds(pl.multiple_of(part * SEG + col * 128, 128), 128),
        ] = value.astype(BF16)

    def pair(ref, i, r, row, col):
        ga, gb = at(gsp, i, row, 0, col), at(gsp, i, row, 1, col)
        ka, kb, k2 = (at(ref, r, row, part, col) for part in range(3))
        return ga * ka + gb * kb, gb * k2 - ga * kb

    @pl.loop(0, (SUB // tile) * cols)
    def _(pos):
        row, col = pos // cols, pos % cols
        for j in range(NSEG):
            re = im = None
            for i in range(j, NSEG):
                a, b = pair(ksp, i, i - j, row, col)
                re, im = (a, b) if re is None else (re + a, im + b)
            put(j, row, 0, col, re)
            put(j, row, 1, col, im)

    y_s[...] = jnp.dot(abuf[...], inv_v[...], preferred_element_type=F32).astype(BF16)
    collect(y_s, y_r, 3)

    lane_sign = sign[:, :128]

    @pl.loop(0, (SUB // tile) * cols)
    def _(pos):
        row, col = pos // cols, pos % cols
        later = None
        for r in reversed(range(NSEG)):
            re = im = None
            for j in range(NSEG - r):
                a, b = pair(csp, j + r, j, row, col)
                re, im = (a, b) if re is None else (re + a, im + b)
            if later is None:
                put(r, row, 0, col, re)
                put(r, row, 1, col, im)
            else:
                put(r, row, 0, col, re + lane_sign * later[0])
                put(r, row, 1, col, im + lane_sign * later[1])
            later = (re, im)

    l_s[...] = jnp.dot(abuf[...], inv_v[...], preferred_element_type=F32).astype(BF16)
    collect(l_s, l_r, 4)

    all_in(y_r, 3)
    out_ref[pl.ds(0, LS)] = y_r[...].astype(F32).T.astype(BF16)
    all_in(l_r, 4)
    out_ref[pl.ds(LS, LS)] = l_r[...].astype(F32).T.astype(BF16)

    all_sent = x_v.at[pl.ds(0, N_CH - 1)]
    pltpu.make_async_copy(all_sent, all_sent, ring_send).wait()
    assert len(keys) == RING_RECV
    for which, block in enumerate((ct_s, tt_s, gt_s, y_s, l_s)):
        all_out(block, which)


def shards(grad_out, out_weight, query_gate, key_branch, value_branch, filter_taps):
    fwd, inv = tables()
    any_spec = pl.BlockSpec(memory_space=pl.ANY)
    vmem_spec = pl.BlockSpec(memory_space=pltpu.VMEM)
    block = (LS, CH)
    turned = (CH, LS)
    local = (NSEG * SUB, SEG)
    both = pl.pallas_call(
        kernel,
        out_shape=pltpu.VMEM((2 * LS, CH), BF16),
        in_specs=[any_spec] * 8,
        out_specs=vmem_spec,
        scratch_shapes=[
            pltpu.VMEM((N_CH, LS, CH), BF16),
            pltpu.VMEM((N_CH, CH, CH), BF16),
            pltpu.VMEM((4, *block), BF16),
            pltpu.VMEM((SEG, 2 * SEG), BF16),
            pltpu.VMEM((2 * SEG, SEG), BF16),
            pltpu.VMEM(turned, F32),
            pltpu.VMEM(turned, BF16),
            pltpu.VMEM(turned, BF16),
            pltpu.VMEM(turned, BF16),
            pltpu.VMEM(turned, F32),
            pltpu.VMEM(local, BF16),
            pltpu.VMEM(local, BF16),
            pltpu.VMEM(local, BF16),
            pltpu.VMEM((NSEG * SUB, 2 * SEG), F32),
            pltpu.VMEM((NSEG * SUB, 3 * SEG), F32),
            pltpu.VMEM((NSEG * SUB, 3 * SEG), F32),
            pltpu.VMEM((NSEG * SUB, 2 * SEG), BF16),
            pltpu.VMEM(local, BF16),
            pltpu.VMEM(local, BF16),
            pltpu.VMEM(turned, BF16),
            pltpu.VMEM(turned, BF16),
            pltpu.SemaphoreType.DMA((4,)),
            pltpu.SemaphoreType.DMA,
            pltpu.SemaphoreType.DMA,
            pltpu.SemaphoreType.DMA((RING_RECV,)),
            pltpu.SemaphoreType.DMA((5,)),
            pltpu.SemaphoreType.DMA((5,)),
        ],
        compiler_params=pltpu.CompilerParams(
            collective_id=0, has_side_effects=True, vmem_limit_bytes=VMEM_GRANT
        ),
        name="hyena_backward",
    )(grad_out, out_weight, query_gate, key_branch, value_branch, filter_taps, fwd, inv)
    conv = both[:LS].astype(F32)
    lag = both[LS:].astype(F32)
    return (
        (conv * value_branch.astype(F32)).astype(BF16),
        (conv * key_branch.astype(F32)).astype(BF16),
        lag * (1.0 / math.sqrt(LS * N_SEQ)),
    )


def solution(mesh):
    spec = P("seq", "ch")
    return jax.shard_map(
        shards,
        mesh=mesh,
        in_specs=(spec, P("ch", None), spec, spec, spec, spec),
        out_specs=(spec, spec, spec),
        check_vma=False,
    )
```

```python
import functools
import math

import jax
import jax.numpy as jnp
import numpy as np
from jax import lax
from jax.experimental import pallas as pl
from jax.experimental.pallas import tpu as pltpu
from jax.sharding import PartitionSpec as P

F32 = jnp.float32
BF16 = jnp.bfloat16
MESH = pl.DeviceIdType.MESH

VMEM_GRANT = 66060288
N_SEQ = 16
N_CH = 16
NZ = 8
LS = 128
CH = 512
SUB = CH // N_SEQ
SEG = 256
NSEG = LS * N_SEQ // SEG


def tables():
    m = 2 * SEG
    t = np.arange(SEG)
    theta = 2.0 * np.pi * ((t[:, None] * t[None, :]) % m) / m
    fwd = np.concatenate([np.cos(theta), np.sin(theta)], 1)
    fwd[:, SEG] = np.where(t % 2 == 0, 1.0, -1.0)
    weight = np.full((m, 1), 2.0 / m)
    weight[0] = weight[SEG] = 1.0 / m
    return jnp.asarray(fwd, BF16), jnp.asarray(weight * fwd.T, BF16)


Z_OFF = (0, -1, -2, -3, 1, 2, 3, -4)
FIRST, SECOND, LAST = 0, 3, 7
CHUNK = LS // 4
ROWS_A = (0, CHUNK)
ROWS_B = (2 * CHUNK, 3 * CHUNK)
EARLY = 1
HOPS = tuple(
    (dx, dy, dc) for dx in (2, 1, 3, 0) for dy in (1, 0) for dc in (0, 1) if dx or dy or dc
)


def kernel(
    go_hbm, w_hbm, q_hbm, key_hbm, val_hbm, taps_hbm, fwd_hbm, inv_hbm,
    out_ref,
    x_v, w_v, in_v, fwd_v, inv_v, acc,
    ct_s, tt_s, gt_s, qt, c_r, t_r, g_r, gsp, ksp, csp, abuf, y_s, l_s, y_r, l_r,
    in_sem, w_sem, ring_send, own_recv, pair_recv, across_recv, a2a_send, a2a_recv,
):
    s = lax.axis_index("seq")
    c = lax.axis_index("ch")
    z, h = lax.div(c, 2), lax.rem(c, 2)

    def ch_of(zz, hh):
        return lax.rem(zz + 2 * NZ, NZ) * 2 + hh

    def upward(zz):
        return lax.rem(lax.div(zz + 2, 4), 2)

    mine = upward(z)
    step_z = 2 * mine - 1
    ahead, behind = ch_of(z + step_z, h), ch_of(z - step_z, h)
    same_ahead = 1 - (mine + upward(lax.div(ahead, 2))) % 2
    same_behind = 1 - (mine + upward(lax.div(behind, 2))) % 2
    across = z * 2 + (1 - h)

    barrier = pltpu.get_barrier_semaphore()
    for peer in (ahead, behind, across):
        pl.semaphore_signal(barrier, inc=1, device_id={"ch": peer}, device_id_type=MESH)
    pair_in_seq, core = lax.div(s, 2), lax.rem(s, 2)
    x, y_lo = lax.div(pair_in_seq, 2), lax.rem(pair_in_seq, 2)

    def pair_of(hop):
        dx, dy, dc = hop
        return lax.rem(x + dx, 4) * 2 + lax.rem(y_lo + dy, 2), lax.rem(core + dc, 2)

    def seq_of(hop):
        pair, of_pair = pair_of(hop)
        return pair * 2 + of_pair

    for hop in HOPS:
        pl.semaphore_signal(
            barrier, inc=1, device_id={"seq": seq_of(hop)}, device_id_type=MESH
        )

    own = pltpu.make_async_copy(go_hbm, x_v.at[0], in_sem.at[0])
    own.start()
    for i, src in enumerate((key_hbm, val_hbm, taps_hbm, q_hbm)):
        pltpu.make_async_copy(src, in_v.at[i], in_sem.at[1]).start()
    for slot in range(N_CH):
        chunk = ch_of(z + step_z * Z_OFF[slot % NZ], h if slot < NZ else 1 - h)
        pltpu.make_async_copy(
            w_hbm.at[:, pl.ds(pl.multiple_of(chunk * CH, CH), CH)], w_v.at[slot], w_sem
        ).start()
    fwd_load = pltpu.make_async_copy(fwd_hbm, fwd_v, in_sem.at[2])
    fwd_load.start()
    inv_load = pltpu.make_async_copy(inv_hbm, inv_v, in_sem.at[3])
    inv_load.start()

    own.wait()
    pl.semaphore_wait(barrier, 3 + N_SEQ - 1)

    def recv_sem(base, slot, row):
        if base == 0:
            return own_recv.at[slot, row // CHUNK]
        return pair_recv.at[slot, row // CHUNK - 2]

    def push(base, src, dst, row, to, send):
        pltpu.make_async_remote_copy(
            src_ref=x_v.at[base + src, pl.ds(row, CHUNK)],
            dst_ref=x_v.at[base + dst, pl.ds(row, CHUNK)],
            send_sem=ring_send.at[send],
            recv_sem=recv_sem(base, dst, row),
            device_id={"ch": to},
            device_id_type=MESH,
        ).start()

    def push_across(slot, row):
        pltpu.make_async_remote_copy(
            src_ref=x_v.at[slot, pl.ds(row, CHUNK)],
            dst_ref=x_v.at[NZ + slot, pl.ds(row, CHUNK)],
            send_sem=ring_send.at[1],
            recv_sem=across_recv.at[slot] if row in ROWS_A else recv_sem(NZ, 0, row),
            device_id={"ch": across},
            device_id_type=MESH,
        ).start()

    def arrived(base, slot, row):
        part = x_v.at[base + slot, pl.ds(row, CHUNK)]
        pltpu.make_async_copy(part, part, recv_sem(base, slot, row)).wait()

    def arrived_across(slot):
        part = x_v.at[NZ + slot, pl.ds(0, 2 * CHUNK)]
        pltpu.make_async_copy(part, part, across_recv.at[slot]).wait()

    def mult(slot):
        acc[...] += lax.dot_general(
            w_v[slot], x_v[slot], (((1,), (1,)), ((), ())), preferred_element_type=F32
        )

    def mult_pair(slot, wait=False):
        @pl.loop(0, 2)
        def _(side):
            if wait:
                arrived_across(slot - NZ + 3 * side)
            mult(slot + 3 * side)

    slot_ahead = FIRST + 3 * (1 - same_ahead)
    slot_behind = FIRST + 3 * same_behind
    goes_on = (same_ahead == 1, same_behind == 0)

    def start_ring(base, row):
        push(base, 0, slot_ahead + 1, row, ahead, 0)
        push(base, 0, slot_behind + 1, row, behind, 0)

    def ring(side, step, base, rows):
        slot = LAST if step == 4 else side + step
        to, there = (ahead, slot_ahead) if side == FIRST else (behind, slot_behind)
        for row in rows:
            arrived(base, slot, row)
            if step < 3:
                push(base, slot, there + step + 1, row, to, 0)
            elif step == 3:

                @pl.when(goes_on[side // 3])
                def _():
                    push(base, slot, LAST, row, to, 2 + side // 3)

            if base == 0 and row in ROWS_A:
                push_across(slot, row)

    def both_sides(step, base, rows):
        for row in rows:
            for side in (FIRST, SECOND)[: 1 if step == 4 else 2]:
                ring(side, step, base, (row,))

    def ring_own(step):
        both_sides(step, 0, ROWS_A)
        both_sides(step, 0, ROWS_B)

    def ring_pair(step):
        both_sides(step, NZ, ROWS_B)

    for row in ROWS_A:
        start_ring(0, row)
    for row in ROWS_B:
        push_across(0, row)
    for row in ROWS_A:
        push_across(0, row)
    for row in ROWS_B:
        start_ring(0, row)

    def scatter(block, recv, which):
        my_row = pl.ds(pl.multiple_of(pair_in_seq * SUB, SUB), SUB)
        my_col = pl.ds(pl.multiple_of(core * LS, LS), LS)
        pltpu.make_async_copy(
            block.at[pl.ds(pl.multiple_of(s * SUB, SUB), SUB)],
            recv.at[my_row, my_col],
            a2a_recv.at[which],
        ).start()
        for hop in HOPS:
            to = seq_of(hop)
            pltpu.make_async_remote_copy(
                src_ref=block.at[pl.ds(pl.multiple_of(to * SUB, SUB), SUB)],
                dst_ref=recv.at[my_row, my_col],
                send_sem=a2a_send.at[which],
                recv_sem=a2a_recv.at[which],
                device_id={"seq": to},
                device_id_type=MESH,
            ).start()

    def collect(block, recv, which):
        my_row = pl.ds(pl.multiple_of(s * SUB, SUB), SUB)

        def piece(pair, of_pair):
            return block.at[
                pl.ds(pl.multiple_of(pair * SUB, SUB), SUB),
                pl.ds(pl.multiple_of(of_pair * LS, LS), LS),
            ]

        pltpu.make_async_copy(piece(pair_in_seq, core), recv.at[my_row], a2a_recv.at[which]).start()
        def give(pair, of_pair):
            pltpu.make_async_remote_copy(
                src_ref=piece(pair, of_pair),
                dst_ref=recv.at[my_row],
                send_sem=a2a_send.at[which],
                recv_sem=a2a_recv.at[which],
                device_id={"seq": pair * 2 + of_pair},
                device_id_type=MESH,
            ).start()

        pl.when(s != EARLY)(lambda: give(EARLY // 2, EARLY % 2))
        for hop in HOPS:
            pl.when(seq_of(hop) != EARLY)(functools.partial(give, *pair_of(hop)))

    def all_in(recv, which):
        pltpu.make_async_copy(recv, recv, a2a_recv.at[which]).wait()

    def all_out(block, which):
        rows_sent = block.shape[0] - block.shape[0] // N_SEQ
        part = block.at[pl.ds(0, rows_sent)]
        pltpu.make_async_copy(part, part, a2a_send.at[which]).wait()

    pltpu.make_async_copy(in_v, in_v, in_sem.at[1]).wait()
    ct_s[...] = (in_v[0].astype(F32) * in_v[1].astype(F32)).T.astype(BF16)
    scatter(ct_s, c_r, 0)
    tt_s[...] = in_v[2].astype(F32).T.astype(BF16)
    scatter(tt_s, t_r, 1)
    qt[...] = in_v[3].astype(F32).T

    sign = jnp.where(
        lax.broadcasted_iota(jnp.int32, (1, SEG), 1) % 2 == 0, 1.0, -1.0
    ).astype(F32)
    first = lax.broadcasted_iota(jnp.int32, (1, SEG), 1) == 0

    ring_own(1)
    for row in ROWS_B:
        arrived(NZ, 0, row)
        start_ring(NZ, row)
    pltpu.make_async_copy(w_v, w_v, w_sem).wait()
    acc[...] = jnp.zeros_like(acc)
    mult(0)
    mult_pair(1)
    ring_own(2)
    ring_pair(1)
    mult_pair(2)
    arrived_across(0)
    mult(8)
    ring_own(3)
    ring_pair(2)

    def put3(ref, cos, sin):
        ref[:, pl.ds(0, SEG)] = cos
        ref[:, pl.ds(SEG, SEG)] = jnp.where(first, 0.0, sin)
        ref[:, pl.ds(2 * SEG, SEG)] = jnp.where(first, sin, cos)

    fwd_load.wait()
    all_in(c_r, 0)
    spec = jnp.dot(c_r[...], fwd_v[...], preferred_element_type=F32)
    put3(csp, spec[:, :SEG], spec[:, SEG:])
    mult_pair(3)
    ring_own(4)
    ring_pair(3)
    all_in(t_r, 1)
    spec = jnp.dot(t_r[...], fwd_v[...], preferred_element_type=F32)
    before = jnp.concatenate([jnp.zeros((SUB, 2 * SEG), F32), spec[:-SUB]], 0)
    put3(
        ksp,
        spec[:, :SEG] + sign * before[:, :SEG],
        spec[:, SEG:] + sign * before[:, SEG:],
    )
    inv_load.wait()
    mult(7)
    mult_pair(NZ + 1, True)
    mult_pair(NZ + 2, True)
    ring_pair(4)
    mult_pair(NZ + 3, True)
    arrived_across(LAST)
    mult(NZ + LAST)

    gt_s[...] = (acc[...] * qt[...]).astype(BF16)
    scatter(gt_s, g_r, 2)
    all_in(g_r, 2)
    gsp[...] = jnp.dot(g_r[...], fwd_v[...], preferred_element_type=F32)

    tile = 8
    spots = [(row, col) for row in range(0, SUB, tile) for col in range(0, SEG, 128)]

    def at(ref, seg, row, col):
        return ref[pl.ds(seg * SUB + row, tile), pl.ds(col, 128)]

    def put(seg, row, col, value):
        abuf[pl.ds(seg * SUB + row, tile), pl.ds(col, 128)] = value.astype(BF16)

    def correlate(ref, row, col):
        g = [(at(gsp, i, row, col), at(gsp, i, row, SEG + col)) for i in range(NSEG)]
        out = [None] * NSEG
        for j in range(NSEG):
            ka, kb, k2 = (at(ref, j, row, part * SEG + col) for part in range(3))
            for i in range(NSEG - j):
                ga, gb = g[i + j]
                re, im = ga * ka + gb * kb, gb * k2 - ga * kb
                out[i] = (re, im) if out[i] is None else (out[i][0] + re, out[i][1] + im)
        return out

    for row, col in spots:
        for j, (re, im) in enumerate(correlate(ksp, row, col)):
            put(j, row, col, re)
            put(j, row, SEG + col, im)

    y_s[...] = jnp.dot(abuf[...], inv_v[...], preferred_element_type=F32).astype(BF16)
    collect(y_s, y_r, 3)

    lane_sign = sign[:, :128]

    for row, col in spots:
        lags = correlate(csp, row, col)
        for r, (re, im) in enumerate(lags):
            if r + 1 < NSEG:
                re += lane_sign * lags[r + 1][0]
                im += lane_sign * lags[r + 1][1]
            put(r, row, col, re)
            put(r, row, SEG + col, im)

    l_s[...] = jnp.dot(abuf[...], inv_v[...], preferred_element_type=F32).astype(BF16)
    collect(l_s, l_r, 4)

    all_in(y_r, 3)
    out_ref[pl.ds(0, LS)] = y_r[...].astype(F32).T.astype(BF16)
    all_in(l_r, 4)
    out_ref[pl.ds(LS, LS)] = l_r[...].astype(F32).T.astype(BF16)

    def drain(part, i):
        pltpu.make_async_copy(part, part, ring_send.at[i]).wait()

    drain(x_v.at[pl.ds(0, 9)], 0)
    drain(x_v.at[pl.ds(0, 9), pl.ds(0, 2 * CHUNK)], 1)
    for side in (0, 1):

        @pl.when(goes_on[side])
        def _():
            drain(x_v.at[pl.ds(0, 3), pl.ds(0, 2 * CHUNK)], 2 + side)

    for which, block in enumerate((ct_s, tt_s, gt_s, y_s, l_s)):
        all_out(block, which)


def shards(grad_out, out_weight, query_gate, key_branch, value_branch, filter_taps):
    fwd, inv = tables()
    any_spec = pl.BlockSpec(memory_space=pl.ANY)
    vmem_spec = pl.BlockSpec(memory_space=pltpu.VMEM)
    block = (LS, CH)
    turned = (CH, LS)
    local = (NSEG * SUB, SEG)
    both = pl.pallas_call(
        kernel,
        out_shape=pltpu.VMEM((2 * LS, CH), BF16),
        in_specs=[any_spec] * 8,
        out_specs=vmem_spec,
        scratch_shapes=[
            pltpu.VMEM((N_CH, LS, CH), BF16),
            pltpu.VMEM((N_CH, CH, CH), BF16),
            pltpu.VMEM((4, *block), BF16),
            pltpu.VMEM((SEG, 2 * SEG), BF16),
            pltpu.VMEM((2 * SEG, SEG), BF16),
            pltpu.VMEM(turned, F32),
            pltpu.VMEM(turned, BF16),
            pltpu.VMEM(turned, BF16),
            pltpu.VMEM(turned, BF16),
            pltpu.VMEM(turned, F32),
            pltpu.VMEM(local, BF16),
            pltpu.VMEM(local, BF16),
            pltpu.VMEM(local, BF16),
            pltpu.VMEM((NSEG * SUB, 2 * SEG), F32),
            pltpu.VMEM((NSEG * SUB, 3 * SEG), F32),
            pltpu.VMEM((NSEG * SUB, 3 * SEG), F32),
            pltpu.VMEM((NSEG * SUB, 2 * SEG), BF16),
            pltpu.VMEM(local, BF16),
            pltpu.VMEM(local, BF16),
            pltpu.VMEM(turned, BF16),
            pltpu.VMEM(turned, BF16),
            pltpu.SemaphoreType.DMA((4,)),
            pltpu.SemaphoreType.DMA,
            pltpu.SemaphoreType.DMA((4,)),
            pltpu.SemaphoreType.DMA((NZ, 4)),
            pltpu.SemaphoreType.DMA((NZ, 2)),
            pltpu.SemaphoreType.DMA((NZ,)),
            pltpu.SemaphoreType.DMA((5,)),
            pltpu.SemaphoreType.DMA((5,)),
        ],
        compiler_params=pltpu.CompilerParams(
            collective_id=0, has_side_effects=True, vmem_limit_bytes=VMEM_GRANT
        ),
        name="hyena_backward",
    )(grad_out, out_weight, query_gate, key_branch, value_branch, filter_taps, fwd, inv)
    conv = both[:LS].astype(F32)
    lag = both[LS:].astype(F32)
    return (
        (conv * value_branch.astype(F32)).astype(BF16),
        (conv * key_branch.astype(F32)).astype(BF16),
        lag * (1.0 / math.sqrt(LS * N_SEQ)),
    )


def solution(mesh):
    spec = P("seq", "ch")
    return jax.shard_map(
        shards,
        mesh=mesh,
        in_specs=(spec, P("ch", None), spec, spec, spec, spec),
        out_specs=(spec, spec, spec),
        check_vma=False,
    )
```

```python
import functools
import math

import jax
import jax.numpy as jnp
import numpy as np
from jax import lax
from jax.experimental import pallas as pl
from jax.experimental.pallas import tpu as pltpu
from jax.sharding import PartitionSpec as P

F32 = jnp.float32
BF16 = jnp.bfloat16
MESH = pl.DeviceIdType.MESH

VMEM_GRANT = 66060288
N_SEQ = 16
N_CH = 16
NZ = 8
LS = 128
CH = 512
SUB = CH // N_SEQ
SEG = 256
NSEG = LS * N_SEQ // SEG


def tables():
    m = 2 * SEG
    t = np.arange(SEG)
    theta = 2.0 * np.pi * ((t[:, None] * t[None, :]) % m) / m
    fwd = np.concatenate([np.cos(theta), np.sin(theta)], 1)
    fwd[:, SEG] = np.where(t % 2 == 0, 1.0, -1.0)
    weight = np.full((m, 1), 2.0 / m)
    weight[0] = weight[SEG] = 1.0 / m
    return jnp.asarray(fwd, BF16), jnp.asarray(weight * fwd.T, BF16)


Z_OFF = (0, -1, -2, -3, 1, 2, 3, -4)
FIRST, SECOND, LAST = 0, 3, 7
CHUNKS = 4
CHUNK = LS // CHUNKS
N_A = 2
ROWS = tuple(range(0, LS, CHUNK))
ROWS_A, ROWS_B = ROWS[:N_A], ROWS[N_A:]
HOPS = tuple(
    (dx, dy, dc) for dx in (2, 1, 3, 0) for dy in (1, 0) for dc in (0, 1) if dx or dy or dc
)


def kernel(
    go_hbm, w_hbm, q_hbm, key_hbm, val_hbm, taps_hbm, fwd_hbm, inv_hbm,
    out_ref,
    x_v, w_v, in_v, fwd_v, inv_v, acc,
    ct_s, tt_s, gt_s, qt, c_r, t_r, g_r, gsp, ksp, csp, abuf, y_s, l_s, y_r, l_r,
    in_sem, w_sem, ring_send, own_recv, pair_recv, across_recv, a2a_send, a2a_recv,
):
    s = lax.axis_index("seq")
    c = lax.axis_index("ch")
    z, h = lax.div(c, 2), lax.rem(c, 2)

    def ch_of(zz, hh):
        return lax.rem(zz + 2 * NZ, NZ) * 2 + hh

    def upward(zz):
        return lax.rem(lax.div(zz + 2, 4), 2)

    mine = upward(z)
    step_z = 2 * mine - 1
    ahead, behind = ch_of(z + step_z, h), ch_of(z - step_z, h)
    same_ahead = 1 - (mine + upward(lax.div(ahead, 2))) % 2
    same_behind = 1 - (mine + upward(lax.div(behind, 2))) % 2
    across = z * 2 + (1 - h)

    barrier = pltpu.get_barrier_semaphore()
    for peer in (ahead, behind, across):
        pl.semaphore_signal(barrier, inc=1, device_id={"ch": peer}, device_id_type=MESH)
    pair_in_seq, core = lax.div(s, 2), lax.rem(s, 2)
    x, y_lo = lax.div(pair_in_seq, 2), lax.rem(pair_in_seq, 2)

    def pair_of(hop):
        dx, dy, dc = hop
        return lax.rem(x + dx, 4) * 2 + lax.rem(y_lo + dy, 2), lax.rem(core + dc, 2)

    def seq_of(hop):
        pair, of_pair = pair_of(hop)
        return pair * 2 + of_pair

    for hop in HOPS:
        pl.semaphore_signal(
            barrier, inc=1, device_id={"seq": seq_of(hop)}, device_id_type=MESH
        )

    own = pltpu.make_async_copy(go_hbm, x_v.at[0], in_sem.at[0])
    own.start()
    for i, src in enumerate((key_hbm, val_hbm, taps_hbm, q_hbm)):
        pltpu.make_async_copy(src, in_v.at[i], in_sem.at[1]).start()
    for slot in range(N_CH):
        chunk = ch_of(z + step_z * Z_OFF[slot % NZ], h if slot < NZ else 1 - h)
        pltpu.make_async_copy(
            w_hbm.at[:, pl.ds(pl.multiple_of(chunk * CH, CH), CH)], w_v.at[slot], w_sem
        ).start()
    fwd_load = pltpu.make_async_copy(fwd_hbm, fwd_v, in_sem.at[2])
    fwd_load.start()
    inv_load = pltpu.make_async_copy(inv_hbm, inv_v, in_sem.at[3])
    inv_load.start()

    own.wait()
    pl.semaphore_wait(barrier, 3 + N_SEQ - 1)

    def recv_sem(base, slot, row):
        if base == 0:
            return own_recv.at[slot, row // CHUNK]
        return pair_recv.at[slot, row // CHUNK - N_A]

    def push(base, src, dst, row, to, send):
        pltpu.make_async_remote_copy(
            src_ref=x_v.at[base + src, pl.ds(row, CHUNK)],
            dst_ref=x_v.at[base + dst, pl.ds(row, CHUNK)],
            send_sem=ring_send.at[send],
            recv_sem=recv_sem(base, dst, row),
            device_id={"ch": to},
            device_id_type=MESH,
        ).start()

    def push_across(slot, row):
        pltpu.make_async_remote_copy(
            src_ref=x_v.at[slot, pl.ds(row, CHUNK)],
            dst_ref=x_v.at[NZ + slot, pl.ds(row, CHUNK)],
            send_sem=ring_send.at[1],
            recv_sem=across_recv.at[slot] if row in ROWS_A else recv_sem(NZ, 0, row),
            device_id={"ch": across},
            device_id_type=MESH,
        ).start()

    def arrived(base, slot, row):
        part = x_v.at[base + slot, pl.ds(row, CHUNK)]
        pltpu.make_async_copy(part, part, recv_sem(base, slot, row)).wait()

    def arrived_across(slot):
        part = x_v.at[NZ + slot, pl.ds(0, N_A * CHUNK)]
        pltpu.make_async_copy(part, part, across_recv.at[slot]).wait()

    def mult(slot):
        acc[...] += lax.dot_general(
            w_v[slot], x_v[slot], (((1,), (1,)), ((), ())), preferred_element_type=F32
        )

    def mult_pair(slot, wait=False):
        @pl.loop(0, 2)
        def _(side):
            if wait:
                arrived_across(slot - NZ + 3 * side)
            mult(slot + 3 * side)

    slot_ahead = FIRST + 3 * (1 - same_ahead)
    slot_behind = FIRST + 3 * same_behind
    goes_on = (same_ahead == 1, same_behind == 0)

    def start_ring(base, row):
        push(base, 0, slot_ahead + 1, row, ahead, 0)
        push(base, 0, slot_behind + 1, row, behind, 0)

    def ring(side, step, base, rows):
        slot = LAST if step == 4 else side + step
        to, there = (ahead, slot_ahead) if side == FIRST else (behind, slot_behind)
        for row in rows:
            arrived(base, slot, row)
            if step < 3:
                push(base, slot, there + step + 1, row, to, 0)
            elif step == 3:

                @pl.when(goes_on[side // 3])
                def _():
                    push(base, slot, LAST, row, to, 2 + side // 3)

            if base == 0 and row in ROWS_A:
                push_across(slot, row)

    def both_sides(step, base, rows):
        for row in rows:
            for side in (FIRST, SECOND)[: 1 if step == 4 else 2]:
                ring(side, step, base, (row,))

    def ring_own(step):
        both_sides(step, 0, ROWS_A)
        both_sides(step, 0, ROWS_B)

    def ring_pair(step):
        both_sides(step, NZ, ROWS_B)

    for row in ROWS_A:
        start_ring(0, row)
    for row in ROWS_B:
        push_across(0, row)
    for row in ROWS_A:
        push_across(0, row)
    for row in ROWS_B:
        start_ring(0, row)

    def scatter(block, recv, which):
        my_row = pl.ds(pl.multiple_of(pair_in_seq * SUB, SUB), SUB)
        my_col = pl.ds(pl.multiple_of(core * LS, LS), LS)
        pltpu.make_async_copy(
            block.at[pl.ds(pl.multiple_of(s * SUB, SUB), SUB)],
            recv.at[my_row, my_col],
            a2a_recv.at[which],
        ).start()
        for hop in HOPS:
            to = seq_of(hop)
            pltpu.make_async_remote_copy(
                src_ref=block.at[pl.ds(pl.multiple_of(to * SUB, SUB), SUB)],
                dst_ref=recv.at[my_row, my_col],
                send_sem=a2a_send.at[which],
                recv_sem=a2a_recv.at[which],
                device_id={"seq": to},
                device_id_type=MESH,
            ).start()

    def piece(block, pair, of_pair):
        return block.at[
            pl.ds(pl.multiple_of(pair * SUB, SUB), SUB),
            pl.ds(pl.multiple_of(of_pair * LS, LS), LS),
        ]

    def give(block, recv, which, pair, of_pair):
        pltpu.make_async_remote_copy(
            src_ref=piece(block, pair, of_pair),
            dst_ref=recv.at[pl.ds(pl.multiple_of(s * SUB, SUB), SUB)],
            send_sem=a2a_send.at[which],
            recv_sem=a2a_recv.at[which],
            device_id={"seq": pair * 2 + of_pair},
            device_id_type=MESH,
        ).start()

    def collect_first(block, recv, which):
        for of_pair in (1, 0):
            pl.when(s != of_pair)(functools.partial(give, block, recv, which, 0, of_pair))

    def collect(block, recv, which):
        for hop in HOPS:
            pair, of_pair = pair_of(hop)
            pl.when(pair != 0)(functools.partial(give, block, recv, which, pair, of_pair))
        pltpu.make_async_copy(
            piece(block, pair_in_seq, core),
            recv.at[pl.ds(pl.multiple_of(s * SUB, SUB), SUB)],
            a2a_recv.at[which],
        ).start()

    def all_in(recv, which):
        pltpu.make_async_copy(recv, recv, a2a_recv.at[which]).wait()

    def all_out(block, which):
        rows_sent = block.shape[0] - block.shape[0] // N_SEQ
        part = block.at[pl.ds(0, rows_sent)]
        pltpu.make_async_copy(part, part, a2a_send.at[which]).wait()

    pltpu.make_async_copy(in_v, in_v, in_sem.at[1]).wait()
    ct_s[...] = (in_v[0].astype(F32) * in_v[1].astype(F32)).T.astype(BF16)
    scatter(ct_s, c_r, 0)
    tt_s[...] = in_v[2].astype(F32).T.astype(BF16)
    scatter(tt_s, t_r, 1)
    qt[...] = in_v[3].astype(F32).T

    sign = jnp.where(
        lax.broadcasted_iota(jnp.int32, (1, SEG), 1) % 2 == 0, 1.0, -1.0
    ).astype(F32)
    first = lax.broadcasted_iota(jnp.int32, (1, SEG), 1) == 0

    ring_own(1)
    for row in ROWS_B:
        arrived(NZ, 0, row)
        start_ring(NZ, row)
    pltpu.make_async_copy(w_v, w_v, w_sem).wait()
    acc[...] = jnp.zeros_like(acc)
    mult(0)
    mult_pair(1)
    ring_own(2)
    ring_pair(1)
    mult_pair(2)
    arrived_across(0)
    mult(8)
    ring_own(3)
    ring_pair(2)

    def put3(ref, cos, sin):
        ref[:, pl.ds(0, SEG)] = cos
        ref[:, pl.ds(SEG, SEG)] = jnp.where(first, 0.0, sin)
        ref[:, pl.ds(2 * SEG, SEG)] = jnp.where(first, sin, cos)

    fwd_load.wait()
    all_in(c_r, 0)
    spec = jnp.dot(c_r[...], fwd_v[...], preferred_element_type=F32)
    put3(csp, spec[:, :SEG], spec[:, SEG:])
    mult_pair(3)
    ring_own(4)
    ring_pair(3)
    all_in(t_r, 1)
    spec = jnp.dot(t_r[...], fwd_v[...], preferred_element_type=F32)
    before = jnp.concatenate([jnp.zeros((SUB, 2 * SEG), F32), spec[:-SUB]], 0)
    put3(
        ksp,
        spec[:, :SEG] + sign * before[:, :SEG],
        spec[:, SEG:] + sign * before[:, SEG:],
    )
    inv_load.wait()
    mult(7)
    mult_pair(NZ + 1, True)
    mult_pair(NZ + 2, True)
    ring_pair(4)
    mult_pair(NZ + 3, True)
    arrived_across(LAST)
    mult(NZ + LAST)

    gt_s[...] = (acc[...] * qt[...]).astype(BF16)
    scatter(gt_s, g_r, 2)
    all_in(g_r, 2)
    gsp[...] = jnp.dot(g_r[...], fwd_v[...], preferred_element_type=F32)

    tile = 8
    spots = [(row, col) for row in range(0, SUB, tile) for col in range(0, SEG, 128)]

    def at(ref, seg, row, col):
        return ref[pl.ds(seg * SUB + row, tile), pl.ds(col, 128)]

    def put(seg, row, col, value):
        abuf[pl.ds(seg * SUB + row, tile), pl.ds(col, 128)] = value.astype(BF16)

    def correlate(ref, row, col, wanted):
        g = [(at(gsp, i, row, col), at(gsp, i, row, SEG + col)) for i in range(NSEG)]
        out = dict.fromkeys(wanted)
        for j in range(NSEG):
            ka, kb, k2 = (at(ref, j, row, part * SEG + col) for part in range(3))
            for i in wanted:
                if i + j < NSEG:
                    ga, gb = g[i + j]
                    re, im = ga * ka + gb * kb, gb * k2 - ga * kb
                    out[i] = (re, im) if out[i] is None else (out[i][0] + re, out[i][1] + im)
        return out

    def grads(segs, base):
        for row, col in spots:
            for j, (re, im) in correlate(ksp, row, col, segs).items():
                put(base + j, row, col, re)
                put(base + j, row, SEG + col, im)

    lane_sign = sign[:, :128]

    def lags(segs, base):
        for row, col in spots:
            sums = correlate(csp, row, col, range(segs[0], min(segs[-1] + 2, NSEG)))
            for r in segs:
                re, im = sums[r]
                if r + 1 < NSEG:
                    re += lane_sign * sums[r + 1][0]
                    im += lane_sign * sums[r + 1][1]
                put(base + r, row, col, re)
                put(base + r, row, SEG + col, im)

    def inverse(rows):
        return jnp.dot(abuf[rows], inv_v[...], preferred_element_type=F32).astype(BF16)

    head, rest = pl.ds(0, SUB), pl.ds(SUB, (NSEG - 1) * SUB)
    grads(range(1), 0)
    lags(range(1), NSEG)
    y_s[head] = inverse(head)
    collect_first(y_s, y_r, 3)
    l_s[head] = inverse(pl.ds(NSEG * SUB, SUB))
    collect_first(l_s, l_r, 4)
    grads(range(1, NSEG), 0)
    y_s[rest] = inverse(rest)
    collect(y_s, y_r, 3)
    lags(range(1, NSEG), 0)
    l_s[rest] = inverse(rest)
    collect(l_s, l_r, 4)

    all_in(y_r, 3)
    out_ref[pl.ds(0, LS)] = y_r[...].astype(F32).T.astype(BF16)
    all_in(l_r, 4)
    out_ref[pl.ds(LS, LS)] = l_r[...].astype(F32).T.astype(BF16)

    def drain(chunks, i):
        rows = next(r for r in range(LS, 0, -16) if chunks * CHUNK % r == 0)
        part = x_v.at[pl.ds(0, chunks * CHUNK // rows), pl.ds(0, rows)]
        pltpu.make_async_copy(part, part, ring_send.at[i]).wait()

    flows = CHUNKS + len(ROWS_B)
    drain(6 * flows, 0)
    drain(NZ * N_A + len(ROWS_B), 1)
    for side in (0, 1):
        pl.when(goes_on[side])(functools.partial(drain, flows, 2 + side))

    for which, block in enumerate((ct_s, tt_s, gt_s, y_s, l_s)):
        all_out(block, which)


def shards(grad_out, out_weight, query_gate, key_branch, value_branch, filter_taps):
    fwd, inv = tables()
    any_spec = pl.BlockSpec(memory_space=pl.ANY)
    vmem_spec = pl.BlockSpec(memory_space=pltpu.VMEM)
    block = (LS, CH)
    turned = (CH, LS)
    local = (NSEG * SUB, SEG)
    both = pl.pallas_call(
        kernel,
        out_shape=pltpu.VMEM((2 * LS, CH), BF16),
        in_specs=[any_spec] * 8,
        out_specs=vmem_spec,
        scratch_shapes=[
            pltpu.VMEM((N_CH, LS, CH), BF16),
            pltpu.VMEM((N_CH, CH, CH), BF16),
            pltpu.VMEM((4, *block), BF16),
            pltpu.VMEM((SEG, 2 * SEG), BF16),
            pltpu.VMEM((2 * SEG, SEG), BF16),
            pltpu.VMEM(turned, F32),
            pltpu.VMEM(turned, BF16),
            pltpu.VMEM(turned, BF16),
            pltpu.VMEM(turned, BF16),
            pltpu.VMEM(turned, F32),
            pltpu.VMEM(local, BF16),
            pltpu.VMEM(local, BF16),
            pltpu.VMEM(local, BF16),
            pltpu.VMEM((NSEG * SUB, 2 * SEG), F32),
            pltpu.VMEM((NSEG * SUB, 3 * SEG), F32),
            pltpu.VMEM((NSEG * SUB, 3 * SEG), F32),
            pltpu.VMEM(((NSEG + 1) * SUB, 2 * SEG), BF16),
            pltpu.VMEM(local, BF16),
            pltpu.VMEM(local, BF16),
            pltpu.VMEM(turned, BF16),
            pltpu.VMEM(turned, BF16),
            pltpu.SemaphoreType.DMA((4,)),
            pltpu.SemaphoreType.DMA,
            pltpu.SemaphoreType.DMA((4,)),
            pltpu.SemaphoreType.DMA((NZ, CHUNKS)),
            pltpu.SemaphoreType.DMA((NZ, CHUNKS - N_A)),
            pltpu.SemaphoreType.DMA((NZ,)),
            pltpu.SemaphoreType.DMA((5,)),
            pltpu.SemaphoreType.DMA((5,)),
        ],
        compiler_params=pltpu.CompilerParams(
            collective_id=0, has_side_effects=True, vmem_limit_bytes=VMEM_GRANT
        ),
        name="hyena_backward",
    )(grad_out, out_weight, query_gate, key_branch, value_branch, filter_taps, fwd, inv)
    conv = both[:LS].astype(F32)
    lag = both[LS:].astype(F32)
    return (
        (conv * value_branch.astype(F32)).astype(BF16),
        (conv * key_branch.astype(F32)).astype(BF16),
        lag * (1.0 / math.sqrt(LS * N_SEQ)),
    )


def solution(mesh):
    spec = P("seq", "ch")
    return jax.shard_map(
        shards,
        mesh=mesh,
        in_specs=(spec, P("ch", None), spec, spec, spec, spec),
        out_specs=(spec, spec, spec),
        check_vma=False,
    )
```

```python
import functools
import math

import jax
import jax.numpy as jnp
import numpy as np
from jax import lax
from jax.experimental import pallas as pl
from jax.experimental.pallas import tpu as pltpu
from jax.sharding import PartitionSpec as P

F32 = jnp.float32
BF16 = jnp.bfloat16
MESH = pl.DeviceIdType.MESH

VMEM_GRANT = 66060288
N_SEQ = 16
N_CH = 16
NZ = 8
LS = 128
CH = 512
SUB = CH // N_SEQ
SEG = 256
NSEG = LS * N_SEQ // SEG


def tables():
    m = 2 * SEG
    t = np.arange(SEG)
    theta = 2.0 * np.pi * ((t[:, None] * t[None, :]) % m) / m
    fwd = np.concatenate([np.cos(theta), np.sin(theta)], 1)
    fwd[:, SEG] = np.where(t % 2 == 0, 1.0, -1.0)
    weight = np.full((m, 1), 2.0 / m)
    weight[0] = weight[SEG] = 1.0 / m
    return jnp.asarray(fwd, BF16), jnp.asarray(weight * fwd.T, BF16)


Z_OFF = (0, -1, -2, -3, 1, 2, 3, -4)
FIRST, SECOND, LAST = 0, 3, 7
CHUNKS = 4
CHUNK = LS // CHUNKS
N_A = 2
ROWS = tuple(range(0, LS, CHUNK))
ROWS_A, ROWS_B = ROWS[:N_A], ROWS[N_A:]
HOPS = tuple(
    (dx, dy, dc) for dx in (2, 1, 3, 0) for dy in (1, 0) for dc in (0, 1) if dx or dy or dc
)


def kernel(
    go_hbm, w_hbm, q_hbm, key_hbm, val_hbm, taps_hbm, fwd_hbm, inv_hbm,
    out_ref,
    x_v, w_v, in_v, fwd_v, inv_v, acc,
    ct_s, tt_s, gt_s, qt, c_r, t_r, g_r, gsp, ksp, csp, abuf, y_s, l_s, y_r, l_r,
    in_sem, w_sem, ring_send, own_recv, pair_recv, across_recv, a2a_send, a2a_recv,
):
    s = lax.axis_index("seq")
    c = lax.axis_index("ch")
    z, h = lax.div(c, 2), lax.rem(c, 2)

    def ch_of(zz, hh):
        return lax.rem(zz + 2 * NZ, NZ) * 2 + hh

    def upward(zz):
        return lax.rem(lax.div(zz + 2, 4), 2)

    mine = upward(z)
    step_z = 2 * mine - 1
    ahead, behind = ch_of(z + step_z, h), ch_of(z - step_z, h)
    same_ahead = 1 - (mine + upward(lax.div(ahead, 2))) % 2
    same_behind = 1 - (mine + upward(lax.div(behind, 2))) % 2
    across = z * 2 + (1 - h)

    barrier = pltpu.get_barrier_semaphore()
    for peer in (ahead, behind, across):
        pl.semaphore_signal(barrier, inc=1, device_id={"ch": peer}, device_id_type=MESH)
    pair_in_seq, core = lax.div(s, 2), lax.rem(s, 2)
    x, y_lo = lax.div(pair_in_seq, 2), lax.rem(pair_in_seq, 2)

    def pair_of(hop):
        dx, dy, dc = hop
        return lax.rem(x + dx, 4) * 2 + lax.rem(y_lo + dy, 2), lax.rem(core + dc, 2)

    def seq_of(hop):
        pair, of_pair = pair_of(hop)
        return pair * 2 + of_pair

    for hop in HOPS:
        pl.semaphore_signal(
            barrier, inc=1, device_id={"seq": seq_of(hop)}, device_id_type=MESH
        )

    own = pltpu.make_async_copy(go_hbm, x_v.at[0], in_sem.at[0])
    own.start()
    for i, src in enumerate((key_hbm, val_hbm, taps_hbm, q_hbm)):
        pltpu.make_async_copy(src, in_v.at[i], in_sem.at[1]).start()
    for slot in range(N_CH):
        chunk = ch_of(z + step_z * Z_OFF[slot % NZ], h if slot < NZ else 1 - h)
        pltpu.make_async_copy(
            w_hbm.at[:, pl.ds(pl.multiple_of(chunk * CH, CH), CH)], w_v.at[slot], w_sem
        ).start()
    fwd_load = pltpu.make_async_copy(fwd_hbm, fwd_v, in_sem.at[2])
    fwd_load.start()
    inv_load = pltpu.make_async_copy(inv_hbm, inv_v, in_sem.at[3])
    inv_load.start()

    own.wait()
    pl.semaphore_wait(barrier, 3 + N_SEQ - 1)

    def recv_sem(base, slot, row):
        if base == 0:
            return own_recv.at[slot, row // CHUNK]
        return pair_recv.at[slot, row // CHUNK - N_A]

    def push(base, src, dst, row, to, send):
        pltpu.make_async_remote_copy(
            src_ref=x_v.at[base + src, pl.ds(row, CHUNK)],
            dst_ref=x_v.at[base + dst, pl.ds(row, CHUNK)],
            send_sem=ring_send.at[send],
            recv_sem=recv_sem(base, dst, row),
            device_id={"ch": to},
            device_id_type=MESH,
        ).start()

    def push_across(slot, row):
        pltpu.make_async_remote_copy(
            src_ref=x_v.at[slot, pl.ds(row, CHUNK)],
            dst_ref=x_v.at[NZ + slot, pl.ds(row, CHUNK)],
            send_sem=ring_send.at[1],
            recv_sem=across_recv.at[slot] if row in ROWS_A else recv_sem(NZ, 0, row),
            device_id={"ch": across},
            device_id_type=MESH,
        ).start()

    def arrived(base, slot, row):
        part = x_v.at[base + slot, pl.ds(row, CHUNK)]
        pltpu.make_async_copy(part, part, recv_sem(base, slot, row)).wait()

    def arrived_across(slot):
        part = x_v.at[NZ + slot, pl.ds(0, N_A * CHUNK)]
        pltpu.make_async_copy(part, part, across_recv.at[slot]).wait()

    def mult(slot):
        acc[...] += lax.dot_general(
            w_v[slot], x_v[slot], (((1,), (1,)), ((), ())), preferred_element_type=F32
        )

    def mult_pair(slot, wait=False):
        @pl.loop(0, 2)
        def _(side):
            if wait:
                arrived_across(slot - NZ + 3 * side)
            mult(slot + 3 * side)

    slot_ahead = FIRST + 3 * (1 - same_ahead)
    slot_behind = FIRST + 3 * same_behind
    goes_on = (same_ahead == 1, same_behind == 0)

    def start_ring(base, row):
        push(base, 0, slot_ahead + 1, row, ahead, 0)
        push(base, 0, slot_behind + 1, row, behind, 0)

    def ring(side, step, base, rows):
        slot = LAST if step == 4 else side + step
        to, there = (ahead, slot_ahead) if side == FIRST else (behind, slot_behind)
        for row in rows:
            arrived(base, slot, row)
            if step < 3:
                push(base, slot, there + step + 1, row, to, 0)
            elif step == 3:

                @pl.when(goes_on[side // 3])
                def _():
                    push(base, slot, LAST, row, to, 2 + side // 3)

            if base == 0 and row in ROWS_A:
                push_across(slot, row)

    def both_sides(step, base, rows):
        for row in rows:
            for side in (FIRST, SECOND)[: 1 if step == 4 else 2]:
                ring(side, step, base, (row,))

    def ring_own(step):
        both_sides(step, 0, ROWS_A)
        both_sides(step, 0, ROWS_B)

    def ring_pair(step):
        both_sides(step, NZ, ROWS_B)

    for row in ROWS_A:
        start_ring(0, row)
    for row in ROWS_B:
        push_across(0, row)
    for row in ROWS_A:
        push_across(0, row)
    for row in ROWS_B:
        start_ring(0, row)

    def scatter(block, recv, which, only_dx=None):
        my_row = pl.ds(pl.multiple_of(pair_in_seq * SUB, SUB), SUB)
        my_col = pl.ds(pl.multiple_of(core * LS, LS), LS)
        if not only_dx:
            pltpu.make_async_copy(
                block.at[pl.ds(pl.multiple_of(s * SUB, SUB), SUB)],
                recv.at[my_row, my_col],
                a2a_recv.at[which],
            ).start()
        for hop in HOPS:
            if only_dx not in (None, hop[0]):
                continue
            to = seq_of(hop)
            pltpu.make_async_remote_copy(
                src_ref=block.at[pl.ds(pl.multiple_of(to * SUB, SUB), SUB)],
                dst_ref=recv.at[my_row, my_col],
                send_sem=a2a_send.at[which],
                recv_sem=a2a_recv.at[which],
                device_id={"seq": to},
                device_id_type=MESH,
            ).start()

    def piece(block, pair, of_pair):
        return block.at[
            pl.ds(pl.multiple_of(pair * SUB, SUB), SUB),
            pl.ds(pl.multiple_of(of_pair * LS, LS), LS),
        ]

    def give(block, recv, which, pair, of_pair):
        pltpu.make_async_remote_copy(
            src_ref=piece(block, pair, of_pair),
            dst_ref=recv.at[pl.ds(pl.multiple_of(s * SUB, SUB), SUB)],
            send_sem=a2a_send.at[which],
            recv_sem=a2a_recv.at[which],
            device_id={"seq": pair * 2 + of_pair},
            device_id_type=MESH,
        ).start()

    def collect_first(block, recv, which):
        for of_pair in (1, 0):
            pl.when(s != of_pair)(functools.partial(give, block, recv, which, 0, of_pair))

    def collect(block, recv, which):
        for hop in HOPS:
            pair, of_pair = pair_of(hop)
            pl.when(pair != 0)(functools.partial(give, block, recv, which, pair, of_pair))
        pltpu.make_async_copy(
            piece(block, pair_in_seq, core),
            recv.at[pl.ds(pl.multiple_of(s * SUB, SUB), SUB)],
            a2a_recv.at[which],
        ).start()

    def all_in(recv, which):
        pltpu.make_async_copy(recv, recv, a2a_recv.at[which]).wait()

    def all_out(block, which):
        rows_sent = block.shape[0] - block.shape[0] // N_SEQ
        part = block.at[pl.ds(0, rows_sent)]
        pltpu.make_async_copy(part, part, a2a_send.at[which]).wait()

    pltpu.make_async_copy(in_v, in_v, in_sem.at[1]).wait()
    ct_s[...] = (in_v[0].astype(F32) * in_v[1].astype(F32)).T.astype(BF16)
    scatter(ct_s, c_r, 0)
    tt_s[...] = in_v[2].astype(F32).T.astype(BF16)
    scatter(tt_s, t_r, 1)
    qt[...] = in_v[3].astype(F32).T

    sign = jnp.where(
        lax.broadcasted_iota(jnp.int32, (1, SEG), 1) % 2 == 0, 1.0, -1.0
    ).astype(F32)
    first = lax.broadcasted_iota(jnp.int32, (1, SEG), 1) == 0

    ring_own(1)
    for row in ROWS_B:
        arrived(NZ, 0, row)
        start_ring(NZ, row)
    pltpu.make_async_copy(w_v, w_v, w_sem).wait()
    acc[...] = jnp.zeros_like(acc)
    mult(0)
    mult_pair(1)
    ring_own(2)
    ring_pair(1)
    mult_pair(2)
    arrived_across(0)
    mult(8)
    def put3(ref, cos, sin):
        ref[:, pl.ds(0, SEG)] = cos
        ref[:, pl.ds(SEG, SEG)] = jnp.where(first, 0.0, sin)
        ref[:, pl.ds(2 * SEG, SEG)] = jnp.where(first, sin, cos)

    fwd_load.wait()
    all_in(c_r, 0)
    spec = jnp.dot(c_r[...], fwd_v[...], preferred_element_type=F32)
    put3(csp, spec[:, :SEG], spec[:, SEG:])
    ring_own(3)
    ring_pair(2)

    all_in(t_r, 1)
    spec = jnp.dot(t_r[...], fwd_v[...], preferred_element_type=F32)
    before = jnp.concatenate([jnp.zeros((SUB, 2 * SEG), F32), spec[:-SUB]], 0)
    put3(
        ksp,
        spec[:, :SEG] + sign * before[:, :SEG],
        spec[:, SEG:] + sign * before[:, SEG:],
    )
    mult_pair(3)
    ring_own(4)
    ring_pair(3)
    inv_load.wait()
    mult(7)
    mult_pair(NZ + 1, True)
    mult_pair(NZ + 2, True)
    mult_pair(NZ + 3, True)
    ring_pair(4)
    arrived_across(LAST)

    for dx in (2, 1, 3, 0):
        part = pl.ds(pl.multiple_of(lax.rem(x + dx, 4) * LS, LS), LS)
        product = acc[part] + lax.dot_general(
            w_v[NZ + LAST, part], x_v[NZ + LAST], (((1,), (1,)), ((), ())),
            preferred_element_type=F32,
        )
        gt_s[part] = (product * qt[part]).astype(BF16)
        scatter(gt_s, g_r, 2, dx)
    all_in(g_r, 2)
    gsp[...] = jnp.dot(g_r[...], fwd_v[...], preferred_element_type=F32)

    tile = 8
    spots = [(row, col) for row in range(0, SUB, tile) for col in range(0, SEG, 128)]

    def at(ref, seg, row, col):
        return ref[pl.ds(seg * SUB + row, tile), pl.ds(col, 128)]

    def put(seg, row, col, value):
        abuf[pl.ds(seg * SUB + row, tile), pl.ds(col, 128)] = value.astype(BF16)

    def correlate(ref, row, col, wanted):
        g = [(at(gsp, i, row, col), at(gsp, i, row, SEG + col)) for i in range(NSEG)]
        out = dict.fromkeys(wanted)
        for j in range(NSEG):
            ka, kb, k2 = (at(ref, j, row, part * SEG + col) for part in range(3))
            for i in wanted:
                if i + j < NSEG:
                    ga, gb = g[i + j]
                    re, im = ga * ka + gb * kb, gb * k2 - ga * kb
                    out[i] = (re, im) if out[i] is None else (out[i][0] + re, out[i][1] + im)
        return out

    def grads(segs, base):
        for row, col in spots:
            for j, (re, im) in correlate(ksp, row, col, segs).items():
                put(base + j, row, col, re)
                put(base + j, row, SEG + col, im)

    lane_sign = sign[:, :128]

    def lags(segs, base):
        for row, col in spots:
            sums = correlate(csp, row, col, range(segs[0], min(segs[-1] + 2, NSEG)))
            for r in segs:
                re, im = sums[r]
                if r + 1 < NSEG:
                    re += lane_sign * sums[r + 1][0]
                    im += lane_sign * sums[r + 1][1]
                put(base + r, row, col, re)
                put(base + r, row, SEG + col, im)

    def inverse(rows):
        return jnp.dot(abuf[rows], inv_v[...], preferred_element_type=F32).astype(BF16)

    head, rest = pl.ds(0, SUB), pl.ds(SUB, (NSEG - 1) * SUB)
    grads(range(1), 0)
    lags(range(1), NSEG)
    y_s[head] = inverse(head)
    collect_first(y_s, y_r, 3)
    l_s[head] = inverse(pl.ds(NSEG * SUB, SUB))
    collect_first(l_s, l_r, 4)
    grads(range(1, NSEG), 0)
    y_s[rest] = inverse(rest)
    collect(y_s, y_r, 3)
    lags(range(1, NSEG), 0)
    l_s[rest] = inverse(rest)
    collect(l_s, l_r, 4)

    all_in(y_r, 3)
    out_ref[pl.ds(0, LS)] = y_r[...].astype(F32).T.astype(BF16)
    all_in(l_r, 4)
    out_ref[pl.ds(LS, LS)] = l_r[...].astype(F32).T.astype(BF16)

    def drain(chunks, i):
        rows = next(r for r in range(LS, 0, -16) if chunks * CHUNK % r == 0)
        part = x_v.at[pl.ds(0, chunks * CHUNK // rows), pl.ds(0, rows)]
        pltpu.make_async_copy(part, part, ring_send.at[i]).wait()

    flows = CHUNKS + len(ROWS_B)
    drain(6 * flows, 0)
    drain(NZ * N_A + len(ROWS_B), 1)
    for side in (0, 1):
        pl.when(goes_on[side])(functools.partial(drain, flows, 2 + side))

    for which, block in enumerate((ct_s, tt_s, gt_s, y_s, l_s)):
        all_out(block, which)


def shards(grad_out, out_weight, query_gate, key_branch, value_branch, filter_taps):
    fwd, inv = tables()
    any_spec = pl.BlockSpec(memory_space=pl.ANY)
    vmem_spec = pl.BlockSpec(memory_space=pltpu.VMEM)
    block = (LS, CH)
    turned = (CH, LS)
    local = (NSEG * SUB, SEG)
    both = pl.pallas_call(
        kernel,
        out_shape=pltpu.VMEM((2 * LS, CH), BF16),
        in_specs=[any_spec] * 8,
        out_specs=vmem_spec,
        scratch_shapes=[
            pltpu.VMEM((N_CH, LS, CH), BF16),
            pltpu.VMEM((N_CH, CH, CH), BF16),
            pltpu.VMEM((4, *block), BF16),
            pltpu.VMEM((SEG, 2 * SEG), BF16),
            pltpu.VMEM((2 * SEG, SEG), BF16),
            pltpu.VMEM(turned, F32),
            pltpu.VMEM(turned, BF16),
            pltpu.VMEM(turned, BF16),
            pltpu.VMEM(turned, BF16),
            pltpu.VMEM(turned, F32),
            pltpu.VMEM(local, BF16),
            pltpu.VMEM(local, BF16),
            pltpu.VMEM(local, BF16),
            pltpu.VMEM((NSEG * SUB, 2 * SEG), F32),
            pltpu.VMEM((NSEG * SUB, 3 * SEG), F32),
            pltpu.VMEM((NSEG * SUB, 3 * SEG), F32),
            pltpu.VMEM(((NSEG + 1) * SUB, 2 * SEG), BF16),
            pltpu.VMEM(local, BF16),
            pltpu.VMEM(local, BF16),
            pltpu.VMEM(turned, BF16),
            pltpu.VMEM(turned, BF16),
            pltpu.SemaphoreType.DMA((4,)),
            pltpu.SemaphoreType.DMA,
            pltpu.SemaphoreType.DMA((4,)),
            pltpu.SemaphoreType.DMA((NZ, CHUNKS)),
            pltpu.SemaphoreType.DMA((NZ, CHUNKS - N_A)),
            pltpu.SemaphoreType.DMA((NZ,)),
            pltpu.SemaphoreType.DMA((5,)),
            pltpu.SemaphoreType.DMA((5,)),
        ],
        compiler_params=pltpu.CompilerParams(
            collective_id=0, has_side_effects=True, vmem_limit_bytes=VMEM_GRANT
        ),
        name="hyena_backward",
    )(grad_out, out_weight, query_gate, key_branch, value_branch, filter_taps, fwd, inv)
    conv = both[:LS].astype(F32)
    lag = both[LS:].astype(F32)
    return (
        (conv * value_branch.astype(F32)).astype(BF16),
        (conv * key_branch.astype(F32)).astype(BF16),
        lag * (1.0 / math.sqrt(LS * N_SEQ)),
    )


def solution(mesh):
    spec = P("seq", "ch")
    return jax.shard_map(
        shards,
        mesh=mesh,
        in_specs=(spec, P("ch", None), spec, spec, spec, spec),
        out_specs=(spec, spec, spec),
        check_vma=False,
    )
```

```python
import functools
import math

import jax
import jax.numpy as jnp
import numpy as np
from jax import lax
from jax.experimental import pallas as pl
from jax.experimental.pallas import tpu as pltpu
from jax.sharding import PartitionSpec as P

F32 = jnp.float32
BF16 = jnp.bfloat16
MESH = pl.DeviceIdType.MESH

VMEM_GRANT = 66060288
N_SEQ = 16
N_CH = 16
NZ = 8
LS = 128
CH = 512
SUB = CH // N_SEQ
SEG = 256
NSEG = LS * N_SEQ // SEG


def tables():
    m = 2 * SEG
    t = np.arange(SEG)
    theta = 2.0 * np.pi * ((t[:, None] * t[None, :]) % m) / m
    fwd = np.concatenate([np.cos(theta), np.sin(theta)], 1)
    fwd[:, SEG] = np.where(t % 2 == 0, 1.0, -1.0)
    weight = np.full((m, 1), 2.0 / m)
    weight[0] = weight[SEG] = 1.0 / m
    return jnp.asarray(fwd, BF16), jnp.asarray(weight * fwd.T, BF16)


Z_OFF = (0, -1, -2, -3, 1, 2, 3, -4)
FIRST, SECOND, LAST = 0, 3, 7
CHUNKS = 4
CHUNK = LS // CHUNKS
N_A = 2
ROWS = tuple(range(0, LS, CHUNK))
ROWS_A, ROWS_B = ROWS[:N_A], ROWS[N_A:]
HOPS = tuple(
    (dx, dy, dc) for dx in (2, 1, 3, 0) for dy in (1, 0) for dc in (0, 1) if dx or dy or dc
)


def kernel(
    go_hbm, w_hbm, q_hbm, key_hbm, val_hbm, taps_hbm, fwd_hbm, inv_hbm,
    out_ref,
    x_v, w_v, in_v, fwd_v, inv_v, acc,
    ct_s, tt_s, gt_s, qt, c_r, t_r, g_r, gsp, ksp, csp, abuf, y_s, l_s, y_r, l_r,
    in_sem, w_sem, ring_send, own_recv, pair_recv, across_recv, a2a_send, a2a_recv,
):
    s = lax.axis_index("seq")
    c = lax.axis_index("ch")
    z, h = lax.div(c, 2), lax.rem(c, 2)

    def ch_of(zz, hh):
        return lax.rem(zz + 2 * NZ, NZ) * 2 + hh

    def upward(zz):
        return lax.rem(lax.div(zz + 2, 4), 2)

    mine = upward(z)
    step_z = 2 * mine - 1
    ahead, behind = ch_of(z + step_z, h), ch_of(z - step_z, h)
    same_ahead = 1 - (mine + upward(lax.div(ahead, 2))) % 2
    same_behind = 1 - (mine + upward(lax.div(behind, 2))) % 2
    across = z * 2 + (1 - h)

    barrier = pltpu.get_barrier_semaphore()
    for peer in (ahead, behind, across):
        pl.semaphore_signal(barrier, inc=1, device_id={"ch": peer}, device_id_type=MESH)
    pair_in_seq, core = lax.div(s, 2), lax.rem(s, 2)
    x, y_lo = lax.div(pair_in_seq, 2), lax.rem(pair_in_seq, 2)

    def pair_of(hop):
        dx, dy, dc = hop
        return lax.rem(x + dx, 4) * 2 + lax.rem(y_lo + dy, 2), lax.rem(core + dc, 2)

    def seq_of(hop):
        pair, of_pair = pair_of(hop)
        return pair * 2 + of_pair

    for hop in HOPS:
        pl.semaphore_signal(
            barrier, inc=1, device_id={"seq": seq_of(hop)}, device_id_type=MESH
        )

    own = pltpu.make_async_copy(go_hbm, x_v.at[0], in_sem.at[0])
    own.start()
    for i, src in enumerate((key_hbm, val_hbm, taps_hbm, q_hbm)):
        pltpu.make_async_copy(src, in_v.at[i], in_sem.at[1]).start()
    for slot in range(N_CH):
        chunk = ch_of(z + step_z * Z_OFF[slot % NZ], h if slot < NZ else 1 - h)
        pltpu.make_async_copy(
            w_hbm.at[:, pl.ds(pl.multiple_of(chunk * CH, CH), CH)], w_v.at[slot], w_sem
        ).start()
    fwd_load = pltpu.make_async_copy(fwd_hbm, fwd_v, in_sem.at[2])
    fwd_load.start()
    inv_load = pltpu.make_async_copy(inv_hbm, inv_v, in_sem.at[3])
    inv_load.start()

    own.wait()
    pl.semaphore_wait(barrier, 3 + N_SEQ - 1)

    def recv_sem(base, slot, row):
        if base == 0:
            return own_recv.at[slot, row // CHUNK]
        return pair_recv.at[slot, row // CHUNK - N_A]

    def push(base, src, dst, row, to, send):
        pltpu.make_async_remote_copy(
            src_ref=x_v.at[base + src, pl.ds(row, CHUNK)],
            dst_ref=x_v.at[base + dst, pl.ds(row, CHUNK)],
            send_sem=ring_send.at[send],
            recv_sem=recv_sem(base, dst, row),
            device_id={"ch": to},
            device_id_type=MESH,
        ).start()

    def push_across(slot, row):
        pltpu.make_async_remote_copy(
            src_ref=x_v.at[slot, pl.ds(row, CHUNK)],
            dst_ref=x_v.at[NZ + slot, pl.ds(row, CHUNK)],
            send_sem=ring_send.at[1],
            recv_sem=across_recv.at[slot] if row in ROWS_A else recv_sem(NZ, 0, row),
            device_id={"ch": across},
            device_id_type=MESH,
        ).start()

    def arrived(base, slot, row):
        part = x_v.at[base + slot, pl.ds(row, CHUNK)]
        pltpu.make_async_copy(part, part, recv_sem(base, slot, row)).wait()

    def arrived_across(slot):
        part = x_v.at[NZ + slot, pl.ds(0, N_A * CHUNK)]
        pltpu.make_async_copy(part, part, across_recv.at[slot]).wait()

    def mult(slot):
        acc[...] += lax.dot_general(
            w_v[slot], x_v[slot], (((1,), (1,)), ((), ())), preferred_element_type=F32
        )

    def mult_pair(slot, wait=False):
        @pl.loop(0, 2)
        def _(side):
            if wait:
                arrived_across(slot - NZ + 3 * side)
            mult(slot + 3 * side)

    slot_ahead = FIRST + 3 * (1 - same_ahead)
    slot_behind = FIRST + 3 * same_behind
    goes_on = (same_ahead == 1, same_behind == 0)

    def start_ring(base, row):
        push(base, 0, slot_ahead + 1, row, ahead, 0)
        push(base, 0, slot_behind + 1, row, behind, 0)

    def ring(side, step, base, rows):
        slot = LAST if step == 4 else side + step
        to, there = (ahead, slot_ahead) if side == FIRST else (behind, slot_behind)
        for row in rows:
            arrived(base, slot, row)
            if step < 3:
                push(base, slot, there + step + 1, row, to, 0)
            elif step == 3:

                @pl.when(goes_on[side // 3])
                def _():
                    push(base, slot, LAST, row, to, 2 + side // 3)

            if base == 0 and row in ROWS_A:
                push_across(slot, row)

    def both_sides(step, base, rows):
        for row in rows:
            for side in (FIRST, SECOND)[: 1 if step == 4 else 2]:
                ring(side, step, base, (row,))

    def ring_own(step):
        both_sides(step, 0, ROWS_A)
        both_sides(step, 0, ROWS_B)

    def ring_pair(step):
        both_sides(step, NZ, ROWS_B)

    for row in ROWS_A:
        start_ring(0, row)
    for row in ROWS_B:
        push_across(0, row)
    for row in ROWS_A:
        push_across(0, row)
    for row in ROWS_B:
        start_ring(0, row)

    def scatter(block, recv, which, only_dx=None):
        my_row = pl.ds(pl.multiple_of(pair_in_seq * SUB, SUB), SUB)
        my_col = pl.ds(pl.multiple_of(core * LS, LS), LS)
        if not only_dx:
            pltpu.make_async_copy(
                block.at[pl.ds(pl.multiple_of(s * SUB, SUB), SUB)],
                recv.at[my_row, my_col],
                a2a_recv.at[which],
            ).start()
        for hop in HOPS:
            if only_dx not in (None, hop[0]):
                continue
            to = seq_of(hop)
            pltpu.make_async_remote_copy(
                src_ref=block.at[pl.ds(pl.multiple_of(to * SUB, SUB), SUB)],
                dst_ref=recv.at[my_row, my_col],
                send_sem=a2a_send.at[which],
                recv_sem=a2a_recv.at[which],
                device_id={"seq": to},
                device_id_type=MESH,
            ).start()

    def piece(block, pair, of_pair):
        return block.at[
            pl.ds(pl.multiple_of(pair * SUB, SUB), SUB),
            pl.ds(pl.multiple_of(of_pair * LS, LS), LS),
        ]

    def give(block, recv, which, pair, of_pair):
        pltpu.make_async_remote_copy(
            src_ref=piece(block, pair, of_pair),
            dst_ref=recv.at[pl.ds(pl.multiple_of(s * SUB, SUB), SUB)],
            send_sem=a2a_send.at[which],
            recv_sem=a2a_recv.at[which],
            device_id={"seq": pair * 2 + of_pair},
            device_id_type=MESH,
        ).start()

    def collect_first(block, recv, which):
        for of_pair in (1, 0):
            pl.when(s != of_pair)(functools.partial(give, block, recv, which, 0, of_pair))

    def collect(block, recv, which):
        for hop in HOPS:
            pair, of_pair = pair_of(hop)
            pl.when(pair != 0)(functools.partial(give, block, recv, which, pair, of_pair))
        pltpu.make_async_copy(
            piece(block, pair_in_seq, core),
            recv.at[pl.ds(pl.multiple_of(s * SUB, SUB), SUB)],
            a2a_recv.at[which],
        ).start()

    def all_in(recv, which):
        pltpu.make_async_copy(recv, recv, a2a_recv.at[which]).wait()

    def all_out(block, which):
        rows_sent = block.shape[0] - block.shape[0] // N_SEQ
        part = block.at[pl.ds(0, rows_sent)]
        pltpu.make_async_copy(part, part, a2a_send.at[which]).wait()

    pltpu.make_async_copy(in_v, in_v, in_sem.at[1]).wait()
    ct_s[...] = (in_v[0].astype(F32) * in_v[1].astype(F32)).T.astype(BF16)
    scatter(ct_s, c_r, 0)
    tt_s[...] = in_v[2].astype(F32).T.astype(BF16)
    scatter(tt_s, t_r, 1)
    qt[...] = in_v[3].astype(F32).T

    sign = jnp.where(
        lax.broadcasted_iota(jnp.int32, (1, SEG), 1) % 2 == 0, 1.0, -1.0
    ).astype(F32)
    first = lax.broadcasted_iota(jnp.int32, (1, SEG), 1) == 0

    ring_own(1)
    for row in ROWS_B:
        arrived(NZ, 0, row)
        start_ring(NZ, row)
    pltpu.make_async_copy(w_v, w_v, w_sem).wait()
    acc[...] = jnp.zeros_like(acc)
    mult(0)
    mult_pair(1)
    ring_own(2)
    ring_pair(1)
    mult_pair(2)
    arrived_across(0)
    mult(8)
    def put3(ref, cos, sin):
        ref[:, pl.ds(0, SEG)] = cos
        ref[:, pl.ds(SEG, SEG)] = jnp.where(first, 0.0, sin)
        ref[:, pl.ds(2 * SEG, SEG)] = jnp.where(first, sin, cos)

    fwd_load.wait()
    all_in(c_r, 0)
    spec = jnp.dot(c_r[...], fwd_v[...], preferred_element_type=F32)
    put3(csp, spec[:, :SEG], spec[:, SEG:])
    ring_own(3)
    ring_pair(2)

    all_in(t_r, 1)
    spec = jnp.dot(t_r[...], fwd_v[...], preferred_element_type=F32)
    before = jnp.concatenate([jnp.zeros((SUB, 2 * SEG), F32), spec[:-SUB]], 0)
    put3(
        ksp,
        spec[:, :SEG] + sign * before[:, :SEG],
        spec[:, SEG:] + sign * before[:, SEG:],
    )
    mult_pair(3)
    ring_own(4)
    ring_pair(3)
    inv_load.wait()
    mult(7)
    mult_pair(NZ + 1, True)
    mult_pair(NZ + 2, True)
    mult_pair(NZ + 3, True)
    ring_pair(4)
    arrived_across(LAST)

    for dx in (2, 1, 3, 0):
        part = pl.ds(pl.multiple_of(lax.rem(x + dx, 4) * LS, LS), LS)
        product = acc[part] + lax.dot_general(
            w_v[NZ + LAST, part], x_v[NZ + LAST], (((1,), (1,)), ((), ())),
            preferred_element_type=F32,
        )
        gt_s[part] = (product * qt[part]).astype(BF16)
        scatter(gt_s, g_r, 2, dx)
    all_in(g_r, 2)
    gsp[...] = jnp.dot(g_r[...], fwd_v[...], preferred_element_type=F32)

    tile = 8
    spots = [(row, col) for row in range(0, SUB, tile) for col in range(0, SEG, 128)]

    def at(ref, seg, row, col):
        return ref[pl.ds(seg * SUB + row, tile), pl.ds(col, 128)]

    def put(seg, row, col, value):
        abuf[pl.ds(seg * SUB + row, tile), pl.ds(col, 128)] = value.astype(BF16)

    def correlate(ref, row, col, wanted):
        g = [(at(gsp, i, row, col), at(gsp, i, row, SEG + col)) for i in range(NSEG)]
        out = dict.fromkeys(wanted)
        for j in range(NSEG):
            ka, kb, k2 = (at(ref, j, row, part * SEG + col) for part in range(3))
            for i in wanted:
                if i + j < NSEG:
                    ga, gb = g[i + j]
                    re, im = ga * ka + gb * kb, gb * k2 - ga * kb
                    out[i] = (re, im) if out[i] is None else (out[i][0] + re, out[i][1] + im)
        return out

    def grads(segs, base):
        for row, col in spots:
            for j, (re, im) in correlate(ksp, row, col, segs).items():
                put(base + j, row, col, re)
                put(base + j, row, SEG + col, im)

    lane_sign = sign[:, :128]

    def lags(segs, base):
        for row, col in spots:
            sums = correlate(csp, row, col, range(segs[0], min(segs[-1] + 2, NSEG)))
            for r in segs:
                re, im = sums[r]
                if r + 1 < NSEG:
                    re += lane_sign * sums[r + 1][0]
                    im += lane_sign * sums[r + 1][1]
                put(base + r, row, col, re)
                put(base + r, row, SEG + col, im)

    def inverse(rows):
        return jnp.dot(abuf[rows], inv_v[...], preferred_element_type=F32).astype(BF16)

    head, rest = pl.ds(0, SUB), pl.ds(SUB, (NSEG - 1) * SUB)
    grads(range(1), 0)
    lags(range(1), NSEG)
    y_s[head] = inverse(head)
    collect_first(y_s, y_r, 3)
    l_s[head] = inverse(pl.ds(NSEG * SUB, SUB))
    collect_first(l_s, l_r, 4)
    grads(range(1, NSEG), 0)
    y_s[rest] = inverse(rest)
    collect(y_s, y_r, 3)
    lags(range(1, NSEG), 0)
    l_s[rest] = inverse(rest)
    collect(l_s, l_r, 4)

    def drain(chunks, i):
        rows = next(r for r in range(LS, 0, -16) if chunks * CHUNK % r == 0)
        part = x_v.at[pl.ds(0, chunks * CHUNK // rows), pl.ds(0, rows)]
        pltpu.make_async_copy(part, part, ring_send.at[i]).wait()

    flows = CHUNKS + len(ROWS_B)
    drain(6 * flows, 0)
    drain(NZ * N_A + len(ROWS_B), 1)
    for side in (0, 1):
        pl.when(goes_on[side])(functools.partial(drain, flows, 2 + side))
    for which, block in enumerate((ct_s, tt_s, gt_s)):
        all_out(block, which)

    all_in(y_r, 3)
    out_ref[pl.ds(0, LS)] = y_r[...].astype(F32).T.astype(BF16)
    all_out(y_s, 3)
    all_in(l_r, 4)
    out_ref[pl.ds(LS, LS)] = l_r[...].astype(F32).T.astype(BF16)
    all_out(l_s, 4)


def shards(grad_out, out_weight, query_gate, key_branch, value_branch, filter_taps):
    fwd, inv = tables()
    any_spec = pl.BlockSpec(memory_space=pl.ANY)
    vmem_spec = pl.BlockSpec(memory_space=pltpu.VMEM)
    block = (LS, CH)
    turned = (CH, LS)
    local = (NSEG * SUB, SEG)
    both = pl.pallas_call(
        kernel,
        out_shape=pltpu.VMEM((2 * LS, CH), BF16),
        in_specs=[any_spec] * 8,
        out_specs=vmem_spec,
        scratch_shapes=[
            pltpu.VMEM((N_CH, LS, CH), BF16),
            pltpu.VMEM((N_CH, CH, CH), BF16),
            pltpu.VMEM((4, *block), BF16),
            pltpu.VMEM((SEG, 2 * SEG), BF16),
            pltpu.VMEM((2 * SEG, SEG), BF16),
            pltpu.VMEM(turned, F32),
            pltpu.VMEM(turned, BF16),
            pltpu.VMEM(turned, BF16),
            pltpu.VMEM(turned, BF16),
            pltpu.VMEM(turned, F32),
            pltpu.VMEM(local, BF16),
            pltpu.VMEM(local, BF16),
            pltpu.VMEM(local, BF16),
            pltpu.VMEM((NSEG * SUB, 2 * SEG), F32),
            pltpu.VMEM((NSEG * SUB, 3 * SEG), F32),
            pltpu.VMEM((NSEG * SUB, 3 * SEG), F32),
            pltpu.VMEM(((NSEG + 1) * SUB, 2 * SEG), BF16),
            pltpu.VMEM(local, BF16),
            pltpu.VMEM(local, BF16),
            pltpu.VMEM(turned, BF16),
            pltpu.VMEM(turned, BF16),
            pltpu.SemaphoreType.DMA((4,)),
            pltpu.SemaphoreType.DMA,
            pltpu.SemaphoreType.DMA((4,)),
            pltpu.SemaphoreType.DMA((NZ, CHUNKS)),
            pltpu.SemaphoreType.DMA((NZ, CHUNKS - N_A)),
            pltpu.SemaphoreType.DMA((NZ,)),
            pltpu.SemaphoreType.DMA((5,)),
            pltpu.SemaphoreType.DMA((5,)),
        ],
        compiler_params=pltpu.CompilerParams(
            collective_id=0, has_side_effects=True, vmem_limit_bytes=VMEM_GRANT
        ),
        name="hyena_backward",
    )(grad_out, out_weight, query_gate, key_branch, value_branch, filter_taps, fwd, inv)
    conv = both[:LS].astype(F32)
    lag = both[LS:].astype(F32)
    return (
        (conv * value_branch.astype(F32)).astype(BF16),
        (conv * key_branch.astype(F32)).astype(BF16),
        lag * (1.0 / math.sqrt(LS * N_SEQ)),
    )


def solution(mesh):
    spec = P("seq", "ch")
    return jax.shard_map(
        shards,
        mesh=mesh,
        in_specs=(spec, P("ch", None), spec, spec, spec, spec),
        out_specs=(spec, spec, spec),
        check_vma=False,
    )
```
